32 devices in a mesh: groups: 2 (over x), wide: 16 (over z, y, core).
Axes of the slice: x: 2, y: 2, z: 4, core: 2. Of those that a mesh axis runs over, the one named last changes fastest.
Arguments:
- alignment_token_ids: int32 [256, 256], P(('groups', 'wide')), parts along dimension 0, may hold values from 0 to 22
- residue_index_offsets: int32 [512], P('groups'), parts along dimension 0, may hold values from 0 to 10240, as said below
- target_residue_feature: float32 [512, 256], P('groups'), parts along dimension 0, may hold values from -6 to 6
- token_embedding_table: float32 [23, 256], replicated, may hold values from -6 to 6
- attention_norm_gain: float32 [256], replicated, may hold values from 0.1 to 1.9
- query_weight: bfloat16 [256, 256], replicated, may hold values from -1 to 1
- key_weight: bfloat16 [256, 256], replicated, may hold values from -25 to 25
- value_weight: bfloat16 [256, 256], replicated, may hold values from -0.375 to 0.375
- gate_weight: bfloat16 [256, 256], replicated, may hold values from -0.375 to 0.375
- gate_offset_bias: float32 [256], replicated, may hold values from -4 to 4
- output_weight: bfloat16 [256, 256], replicated, may hold values from -0.375 to 0.375
- relative_position_table: float32 [65, 8], replicated, may hold values from -4 to 4
- product_norm_gain: float32 [256], replicated, may hold values from 0.1 to 1.9
- left_weight: bfloat16 [256, 32], replicated, may hold values from -0.375 to 0.375
- right_weight: bfloat16 [256, 32], replicated, may hold values from -0.375 to 0.375
- pair_weight: bfloat16 [1024, 128], replicated, may hold values from -0.375 to 0.375
- pair_projection_bias: float32 [128], replicated, may hold values from -3 to 3
Outputs:
- alignment_updated: float32 [256, 256, 256], P(('groups', 'wide')), parts along dimension 0
- pair: float32 [512, 256, 128], P(('groups', 'wide')), parts along dimension 0
The draws below stay inside these ranges and needn't reach their ends.
There are 2 independent parts, one for each index of `groups`. The reference program is written for one: setup_inputs(seed, part) draws one part's arguments, and reference() takes and returns one part's arrays. A program takes and returns all parts, laid end to end along the dimension named above; an argument that names none is the same for every part. Nothing has to cross between parts.
Inputs may be any that keep to these rules, and one draw needn't show every extreme that they name: `residue_index_offsets`: rises by 1 from residue to residue within a chain and by more at chain breaks; the first entry is 0 and the last is 10240.
All inputs are finite; a program needn't handle non-finite values.
Results may differ from the reference program's by a relative error of at most 0.0045.
Values may be sent and summed in bfloat16 or wider, within the bound.
No kernel may reach another device: no remote copies, remote signals or barrier semaphores. Data moves between devices by JAX's collectives and lax.ppermute only.
A program may use at most 128 MiB of HBM per device.

```python
import math
import jax
import jax.numpy as jnp
import numpy as np
from jax import lax

FEATURE_WIDTH = 256
H = 8
DH = 32
F = 32
P_SIZE = 128
TOKEN_CLASSES = 23
REACH = 32
SEQUENCE_COUNT = 128
RESIDUE_COUNT = 256


def query_key(key):
    first = jnp.clip(jax.random.normal(jax.random.fold_in(key, 101), (FEATURE_WIDTH, H * DH), jnp.float32), -6.0, 6.0) / FEATURE_WIDTH ** 0.5
    second = jnp.clip(jax.random.normal(jax.random.fold_in(key, 202), (FEATURE_WIDTH, H * DH), jnp.float32), -6.0, 6.0) / FEATURE_WIDTH ** 0.5
    return (first, second)


def draw_query_weight(key, part):
    first, second = query_key(key)
    return first.astype(jnp.bfloat16)


def draw_key_weight(key, part):
    first, second = query_key(key)
    result = second
    return result.astype(jnp.bfloat16)


def draw_residue_index_offsets(key, part):
    chance = jax.random.randint(jax.random.fold_in(key, 7), (RESIDUE_COUNT,), 0, 64)
    breaks = jax.random.randint(jax.random.fold_in(key, 8), (RESIDUE_COUNT,), 2, 40)
    stepping = jnp.where(chance == 0, breaks, 1)
    stepping = jnp.where(jnp.arange(RESIDUE_COUNT) == 0, 0, stepping)
    positions = jnp.cumsum(stepping).astype(jnp.int32)
    positions = jnp.where(jnp.arange(RESIDUE_COUNT) == RESIDUE_COUNT - 1, 40 * RESIDUE_COUNT, positions)
    return positions.astype(jnp.int32)


def plant(values, stream_key, least, top_value):
    longest = values.shape.index(max(values.shape))
    spots = []
    for shift in (0, 1):
        where = [jax.random.randint(jax.random.fold_in(stream_key, axis), (), 0, length) for axis, length in enumerate(values.shape)]
        where[longest] = (where[longest] + shift) % values.shape[longest]
        spots.append(tuple(where))
    return values.at[spots[0]].set(least).at[spots[1]].set(top_value)


def rank_table(count, lean):
    portions = [(1 << 20) // math.isqrt(grade ** lean) + 1 for grade in range(1, count + 1)]
    scale = 1 + sum(portions) // (1 << 30)
    return np.cumsum(np.array([max(1, weight // scale) for weight in portions]))


def ranked_ids(key, dims, amount, lean):
    grid = rank_table(amount, lean)
    pick = jax.random.randint(jax.random.fold_in(key, 1), dims, 0, int(grid[amount - 1]))
    rank = jnp.searchsorted(jnp.asarray(grid, jnp.int32), pick, side="right")
    return jax.random.permutation(jax.random.fold_in(key, 2), amount)[rank].astype(jnp.int32)


def gaussian(own_key, shape, scale, most, kind=jnp.bfloat16):
    entries = jax.random.normal(own_key, shape, jnp.float32) * scale
    return jnp.minimum(jnp.maximum(entries, -most), most).astype(kind)


def setup_inputs(seed: int = 0, part: int = 0) -> dict:
    arg_keys = jax.random.split(jax.random.key(seed), 18)
    part_splits = jax.random.split(jax.random.fold_in(arg_keys[17], part), 18)
    return {
        "alignment_token_ids": plant(ranked_ids(part_splits[0], (SEQUENCE_COUNT, RESIDUE_COUNT), TOKEN_CLASSES, 2), jax.random.fold_in(part_splits[0], 3), 0, TOKEN_CLASSES - 1).astype(jnp.int32),
        "residue_index_offsets": draw_residue_index_offsets(jax.random.fold_in(jax.random.fold_in(arg_keys[17], part), 71), part),
        "target_residue_feature": gaussian(part_splits[2], (RESIDUE_COUNT, FEATURE_WIDTH), 1.0, 6.0, jnp.float32),
        "token_embedding_table": gaussian(arg_keys[3], (TOKEN_CLASSES, FEATURE_WIDTH), 1.0, 6.0, jnp.float32),
        "attention_norm_gain": jnp.clip(1.0 + 0.18 * jax.random.normal(arg_keys[4], (FEATURE_WIDTH,), jnp.float32), 0.1, 1.9),
        "query_weight": draw_query_weight(jax.random.fold_in(arg_keys[17], 71), part),
        "key_weight": draw_key_weight(jax.random.fold_in(arg_keys[17], 71), part),
        "value_weight": gaussian(arg_keys[7], (FEATURE_WIDTH, H * DH), FEATURE_WIDTH ** -0.5, 0.375),
        "gate_weight": gaussian(arg_keys[8], (FEATURE_WIDTH, H * DH), FEATURE_WIDTH ** -0.5, 0.375),
        "gate_offset_bias": gaussian(arg_keys[9], (H * DH,), 1.0, 4.0, jnp.float32),
        "output_weight": gaussian(arg_keys[10], (H * DH, FEATURE_WIDTH), (H * DH) ** -0.5, 0.375),
        "relative_position_table": gaussian(arg_keys[11], (2 * REACH + 1, H), 1.0, 4.0, jnp.float32),
        "product_norm_gain": jnp.clip(1.0 + 0.18 * jax.random.normal(arg_keys[12], (FEATURE_WIDTH,), jnp.float32), 0.1, 1.9),
        "left_weight": gaussian(arg_keys[13], (FEATURE_WIDTH, F), FEATURE_WIDTH ** -0.5, 0.375),
        "right_weight": gaussian(arg_keys[14], (FEATURE_WIDTH, F), FEATURE_WIDTH ** -0.5, 0.375),
        "pair_weight": gaussian(arg_keys[15], (F * F, P_SIZE), (F * F // 4) ** -0.5, 0.375),
        "pair_projection_bias": gaussian(arg_keys[16], (P_SIZE,), 0.5, 3.0, jnp.float32),
    }


def layer_normalize(values, gain):
    center = lax.optimization_barrier(jnp.mean(values, axis=-1, keepdims=True))
    centred = values - center
    spread = lax.optimization_barrier(jnp.mean(centred * centred, axis=-1, keepdims=True))
    return centred * lax.rsqrt(spread + 1e-05) * gain

def reference(alignment_token_ids, residue_index_offsets, target_residue_feature, token_embedding_table, attention_norm_gain, query_weight, key_weight, value_weight, gate_weight, gate_offset_bias, output_weight, relative_position_table, product_norm_gain, left_weight, right_weight, pair_weight, pair_projection_bias):
    alignment_initial = token_embedding_table[alignment_token_ids] + target_residue_feature[None, :, :]
    offsets = jnp.clip(residue_index_offsets[None, :] - residue_index_offsets[:, None], -REACH, REACH) + REACH
    offset_bias = jnp.transpose(relative_position_table[offsets], (2, 0, 1))

    def row_attention_step(row):
        normed = layer_normalize(row, attention_norm_gain).astype(jnp.bfloat16)
        query = (jnp.dot(normed, query_weight, preferred_element_type=jnp.float32) / DH ** 0.5).astype(jnp.bfloat16)
        keys = jnp.dot(normed, key_weight, preferred_element_type=jnp.float32).astype(jnp.bfloat16)
        values = jnp.dot(normed, value_weight, preferred_element_type=jnp.float32).astype(jnp.bfloat16)
        gate = jax.nn.sigmoid(jnp.dot(normed, gate_weight, preferred_element_type=jnp.float32) + gate_offset_bias)
        query_heads = query.reshape(RESIDUE_COUNT, H, DH).astype(jnp.float32)
        key_heads = keys.reshape(RESIDUE_COUNT, H, DH).astype(jnp.float32)
        value_heads = values.reshape(RESIDUE_COUNT, H, DH).astype(jnp.float32)
        scores = jnp.einsum('ihd,jhd->hij', query_heads, key_heads, precision=lax.Precision.HIGHEST) + offset_bias
        scores = scores - lax.optimization_barrier(jnp.max(scores, axis=-1, keepdims=True))
        expo = jnp.exp(scores)
        weights = (expo / lax.optimization_barrier(jnp.sum(expo, axis=-1, keepdims=True))).astype(jnp.bfloat16)
        mixed = jnp.einsum('hij,jhd->ihd', weights.astype(jnp.float32), value_heads, precision=lax.Precision.HIGHEST)
        mixed = (mixed.reshape(RESIDUE_COUNT, H * DH) * gate).astype(jnp.bfloat16)
        return row + jnp.dot(mixed, output_weight, preferred_element_type=jnp.float32)
    alignment_updated = lax.map(row_attention_step, alignment_initial)
    normalized_second = layer_normalize(alignment_updated, product_norm_gain).astype(jnp.bfloat16).reshape(SEQUENCE_COUNT * RESIDUE_COUNT, FEATURE_WIDTH)
    left = jnp.dot(normalized_second, left_weight, preferred_element_type=jnp.float32).astype(jnp.bfloat16).reshape(SEQUENCE_COUNT, RESIDUE_COUNT, F)
    right = jnp.dot(normalized_second, right_weight, preferred_element_type=jnp.float32).astype(jnp.bfloat16).reshape(SEQUENCE_COUNT, RESIDUE_COUNT, F)
    right_wide = right.astype(jnp.float32)
    blocks = jnp.transpose(left.reshape(SEQUENCE_COUNT, RESIDUE_COUNT // 16, 16, F), (1, 0, 2, 3))

    def rows(block):
        outer = jnp.einsum('sic,sje->ijce', block.astype(jnp.float32), right_wide, precision=lax.Precision.HIGHEST) / SEQUENCE_COUNT
        flat = outer.reshape(16 * RESIDUE_COUNT, F * F).astype(jnp.bfloat16)
        return (jnp.dot(flat, pair_weight, preferred_element_type=jnp.float32) + pair_projection_bias).reshape(16, RESIDUE_COUNT, P_SIZE)
    pair = lax.map(rows, blocks).reshape(RESIDUE_COUNT, RESIDUE_COUNT, P_SIZE)
    return (alignment_updated, pair)
```

```python
import functools

import jax
import jax.numpy as jnp
from jax import lax
from jax.experimental import pallas as pl
from jax.experimental.pallas import tpu as pltpu
from jax.sharding import PartitionSpec as P

REACH = 32
LANES = 128
F32 = jnp.float32
BF16 = jnp.bfloat16


def dot(a, b, axes):
    return lax.dot_general(a, b, (axes, ((), ())), preferred_element_type=F32)


def normalize(values, gain):
    center = jnp.mean(values, axis=-1, keepdims=True)
    centred = values - center
    spread = jnp.mean(centred * centred, axis=-1, keepdims=True)
    return centred * lax.rsqrt(spread + 1e-05) * gain


def attention_kernel(
    heads,
    tokens_ref,
    offsets_ref,
    target_ref,
    embed_ref,
    gain_ref,
    query_ref,
    key_ref,
    value_ref,
    gate_ref,
    gate_bias_ref,
    output_ref,
    relative_ref,
    gain_two_ref,
    left_ref,
    right_ref,
    updated_ref,
    left_out_ref,
    right_out_ref,
    bias_scr,
    relative_scr,
    embed_scr,
    left_scr,
    right_scr,
    weights_scr,
    mixer_scr,
    normed_scr,
    factor_scr,
):
    step = pl.program_id(0)
    sequences, residues = tokens_ref.shape
    features = target_ref.shape[1]
    head_size = query_ref.shape[1] // heads
    packed = LANES // head_size
    groups = heads // packed
    classes = embed_ref.shape[0]
    padded = embed_scr.shape[0] // 3
    width = left_ref.shape[1]
    bins = relative_ref.shape[0]
    owned = left_out_ref.shape[2] // width
    owners = residues // owned

    @pl.when(step == 0)
    def prepare():
        relative_scr[...] = jnp.zeros_like(relative_scr)
        relative_scr[0:bins, 0:heads] = relative_ref[...]
        table = relative_scr[...].T
        row = offsets_ref[...]
        column = jnp.broadcast_to(row, (LANES, residues)).T
        for block in range(residues // LANES):
            lanes = slice(block * LANES, (block + 1) * LANES)
            index = jnp.clip(row[:, lanes] - column, -REACH, REACH) + REACH
            for head in range(heads):
                source = jnp.broadcast_to(table[head : head + 1, :], (residues, LANES))
                bias_scr[head, :, lanes] = jnp.take_along_axis(source, index, axis=1)
        embed_scr[...] = jnp.zeros_like(embed_scr)
        embed = embed_ref[...]
        high = embed.astype(BF16)
        rest = embed - high.astype(F32)
        middle = rest.astype(BF16)
        low = (rest - middle.astype(F32)).astype(BF16)
        for part, piece in enumerate((high, middle, low)):
            embed_scr[part * padded : part * padded + classes, :] = piece
        left_scr[...] = jnp.zeros_like(left_scr)
        for place in range(LANES // width):
            left_scr[place, :, place * width : (place + 1) * width] = left_ref[...]
        right_scr[...] = right_ref[...].astype(F32).T.astype(BF16)

    tokens = tokens_ref[pl.ds(step, 1), :]
    classes_iota = lax.broadcasted_iota(jnp.int32, (padded, residues), 0)
    onehot = (classes_iota == tokens).astype(F32).astype(BF16)
    onehot = jnp.concatenate([onehot, onehot, onehot], axis=0)
    initial = dot(onehot, embed_scr[...], ((0,), (0,))) + target_ref[...]
    normed = normalize(initial, gain_ref[...]).astype(BF16)
    query = (dot(normed, query_ref[...], ((1,), (0,))) * (1.0 / head_size**0.5)).astype(BF16)
    keys = dot(normed, key_ref[...], ((1,), (0,))).astype(BF16)
    values = dot(normed, value_ref[...], ((1,), (0,))).astype(BF16)
    place = lax.broadcasted_iota(jnp.int32, (1, LANES), 1) // head_size
    mixed = []
    for group in range(groups):
        lanes = slice(group * LANES, (group + 1) * LANES)
        for member in range(packed):
            mine = place == member
            rows = slice(member * residues, (member + 1) * residues)
            one_query = jnp.where(mine, query[:, lanes], jnp.zeros((), BF16))
            scores = dot(one_query, keys[:, lanes], ((1,), (1,))) + bias_scr[group * packed + member]
            expo = jnp.exp(scores - jnp.max(scores, axis=-1, keepdims=True))
            weights_scr[:, rows] = expo.astype(BF16)
            mixer_scr[rows, 0:LANES] = jnp.where(mine, values[:, lanes], jnp.zeros((), BF16))
            mixer_scr[rows, LANES:] = jnp.broadcast_to(
                jnp.where(mine, jnp.ones((), BF16), jnp.zeros((), BF16)), (residues, LANES)
            )
        both = dot(weights_scr[...], mixer_scr[...], ((1,), (0,)))
        mixed.append(both[:, :LANES] / both[:, LANES:])
    gate = jax.nn.sigmoid(dot(normed, gate_ref[...], ((1,), (0,))) + gate_bias_ref[...])
    mixed = (jnp.concatenate(mixed, axis=1) * gate).astype(BF16)
    updated = initial + dot(mixed, output_ref[...], ((1,), (0,)))
    updated_ref[0] = updated
    normed_two = normalize(updated, gain_two_ref[...])
    normed_scr[:, pl.ds(step, 1), :] = normed_two[:, None, :]
    factor_scr[:, pl.ds(step, 1), :] = dot(
        right_scr[...], normed_two.astype(BF16), ((1,), (1,))
    )[:, None, :]

    @pl.when(step == pl.num_programs(0) - 1)
    def finish():
        right_out_ref[...] = factor_scr[...].astype(BF16)
        by_owner = normed_scr.reshape(owners, owned, sequences, features)
        count = LANES // width
        for quarter in range(owned // count):
            total = jnp.zeros((owners * sequences, LANES), F32)
            for place in range(count):
                rows = by_owner[:, quarter * count + place].reshape(owners * sequences, features)
                total += dot(rows.astype(BF16), left_scr[place], ((1,), (0,)))
            left_out_ref[:, :, quarter * LANES : (quarter + 1) * LANES] = total.astype(BF16).reshape(
                owners, sequences, LANES
            )


def attention(
    tokens,
    offsets,
    target,
    embed,
    gain,
    query_weight,
    key_weight,
    value_weight,
    gate_weight,
    gate_bias,
    output_weight,
    relative,
    gain_two,
    left_weight,
    right_weight,
    owners,
):
    sequences, residues = tokens.shape
    features = target.shape[1]
    heads = relative.shape[1]
    head_size = query_weight.shape[1] // heads
    packed = LANES // head_size
    width = left_weight.shape[1]
    owned = residues // owners
    padded = -(-embed.shape[0] // 32) * 32
    operands = (
        tokens,
        offsets.reshape(1, -1),
        target,
        embed,
        gain.reshape(1, -1),
        query_weight,
        key_weight,
        value_weight,
        gate_weight,
        gate_bias.reshape(1, -1),
        output_weight,
        relative,
        gain_two.reshape(1, -1),
        left_weight,
        right_weight,
    )
    whole = lambda x: pl.BlockSpec(x.shape, lambda s, n=x.ndim: (0,) * n)
    outs = (
        jax.ShapeDtypeStruct((sequences, residues, features), F32),
        jax.ShapeDtypeStruct((owners, sequences, owned * width), BF16),
        jax.ShapeDtypeStruct((width, sequences, residues), BF16),
    )
    return pl.pallas_call(
        functools.partial(attention_kernel, heads),
        grid=(sequences,),
        in_specs=[whole(x) for x in operands],
        out_specs=(
            pl.BlockSpec((1, residues, features), lambda s: (s, 0, 0)),
            whole(outs[1]),
            whole(outs[2]),
        ),
        out_shape=outs,
        scratch_shapes=[
            pltpu.VMEM((heads, residues, residues), F32),
            pltpu.VMEM((LANES, LANES), F32),
            pltpu.VMEM((3 * padded, features), BF16),
            pltpu.VMEM((LANES // width, features, LANES), BF16),
            pltpu.VMEM((width, features), BF16),
            pltpu.VMEM((residues, packed * residues), BF16),
            pltpu.VMEM((packed * residues, 2 * LANES), BF16),
            pltpu.VMEM((residues, sequences, features), F32),
            pltpu.VMEM((width, sequences, residues), F32),
        ],
        name="attention",
    )(*operands)


def pair_kernel(total, left_ref, right_ref, weight_ref, bias_ref, out_ref, outer_scr, weight_scr, wide_scr):
    width, sequences, residues = right_ref.shape
    block = out_ref.shape[0]
    channels = weight_ref.shape[1]

    @pl.when(pl.program_id(0) == 0)
    def prepare():
        wide_scr[...] = weight_ref[...].astype(F32)
        for e in range(width):
            piece = wide_scr[pl.ds(e, width, stride=width), :]
            weight_scr[:, e * width : (e + 1) * width] = piece.T.astype(BF16)

    left = left_ref[...].astype(F32).T.astype(BF16)
    for e in range(width):
        product = dot(left, right_ref[e], ((1,), (0,))).astype(BF16)
        outer_scr[:, e * width : (e + 1) * width, :] = product.reshape(block, width, residues)
    for i in range(block):
        projected = dot(weight_scr[...], outer_scr[i], ((1,), (0,)))
        out_ref[i] = projected.T * (1.0 / total) + bias_ref[...]


def pair_features(left, right, weight, bias, blocks):
    width, total, residues = right.shape
    owned = left.shape[1] // width
    block = owned // blocks
    channels = weight.shape[1]
    return pl.pallas_call(
        functools.partial(pair_kernel, total),
        grid=(blocks,),
        in_specs=[
            pl.BlockSpec((total, block * width), lambda i: (0, i)),
            pl.BlockSpec(right.shape, lambda i: (0, 0, 0)),
            pl.BlockSpec(weight.shape, lambda i: (0, 0)),
            pl.BlockSpec((1, channels), lambda i: (0, 0)),
        ],
        out_specs=pl.BlockSpec((block, residues, channels), lambda i: (i, 0, 0)),
        out_shape=jax.ShapeDtypeStruct((owned, residues, channels), F32),
        scratch_shapes=[
            pltpu.VMEM((block, width * width, residues), BF16),
            pltpu.VMEM((channels, width * width), BF16),
            pltpu.VMEM(weight.shape, F32),
        ],
        name="pair",
    )(left, right, weight, bias.reshape(1, -1))


def shards(
    alignment_token_ids,
    residue_index_offsets,
    target_residue_feature,
    token_embedding_table,
    attention_norm_gain,
    query_weight,
    key_weight,
    value_weight,
    gate_weight,
    gate_offset_bias,
    output_weight,
    relative_position_table,
    product_norm_gain,
    left_weight,
    right_weight,
    pair_weight,
    pair_projection_bias,
):
    devices = lax.axis_size("wide")
    updated, left, right = attention(
        alignment_token_ids,
        residue_index_offsets,
        target_residue_feature,
        token_embedding_table,
        attention_norm_gain,
        query_weight,
        key_weight,
        value_weight,
        gate_weight,
        gate_offset_bias,
        output_weight,
        relative_position_table,
        product_norm_gain,
        left_weight,
        right_weight,
        devices,
    )
    left_owned = lax.all_to_all(left, "wide", split_axis=0, concat_axis=0, tiled=True)
    left_owned = left_owned.reshape(-1, left_owned.shape[2])
    right_whole = lax.all_gather(right, "wide", axis=1, tiled=True)
    pair = pair_features(left_owned, right_whole, pair_weight, pair_projection_bias, 2)
    return (updated, pair)


def solution(mesh):
    placed = (P(("groups", "wide"), None), P("groups"), P("groups", None)) + (P(),) * 14
    return jax.shard_map(
        shards,
        mesh=mesh,
        in_specs=placed,
        out_specs=(P(("groups", "wide"), None, None), P(("groups", "wide"), None, None)),
        check_vma=False,
    )
```

```python
import functools

import jax
import jax.numpy as jnp
from jax import lax
from jax.experimental import pallas as pl
from jax.experimental.pallas import tpu as pltpu
from jax.sharding import PartitionSpec as P

REACH = 32
LANES = 128
F32 = jnp.float32
BF16 = jnp.bfloat16


def dot(a, b, axes):
    return lax.dot_general(a, b, (axes, ((), ())), preferred_element_type=F32)


def normalize(values, gain):
    center = jnp.mean(values, axis=-1, keepdims=True)
    centred = values - center
    spread = jnp.mean(centred * centred, axis=-1, keepdims=True)
    return centred * lax.rsqrt(spread + 1e-05) * gain


def attention_kernel(
    heads,
    owners,
    outer,
    tokens_ref,
    offsets_ref,
    target_ref,
    embed_ref,
    gain_ref,
    query_ref,
    key_ref,
    value_ref,
    gate_ref,
    gate_bias_ref,
    output_ref,
    relative_ref,
    gain_two_ref,
    left_ref,
    right_ref,
    updated_ref,
    *rest_refs,
):
    message_refs = rest_refs[:outer]
    (
        bias_scr,
        relative_scr,
        embed_scr,
        left_scr,
        weights_scr,
        mixer_scr,
        normed_scr,
        factor_scr,
        owner_scr,
    ) = rest_refs[outer:]
    step = pl.program_id(0)
    sequences, residues = tokens_ref.shape
    features = target_ref.shape[1]
    head_size = query_ref.shape[1] // heads
    packed = LANES // head_size
    groups = heads // packed
    classes = embed_ref.shape[0]
    padded = embed_scr.shape[0] // 3
    width = left_ref.shape[0]
    bins = relative_ref.shape[1]
    inner = owners // outer
    owned = residues // owners
    slabs = owned * width // residues

    @pl.when(step == 0)
    def prepare():
        relative_scr[...] = jnp.zeros_like(relative_scr)
        relative_scr[0:heads, 0:bins] = relative_ref[...]
        table = relative_scr[...]
        row = offsets_ref[...]
        column = jnp.broadcast_to(row, (LANES, residues)).T
        for block in range(residues // LANES):
            lanes = slice(block * LANES, (block + 1) * LANES)
            index = jnp.clip(row[:, lanes] - column, -REACH, REACH) + REACH
            for head in range(heads):
                source = jnp.broadcast_to(table[head : head + 1, :], (residues, LANES))
                bias_scr[head, :, lanes] = jnp.take_along_axis(source, index, axis=1)
        embed_scr[...] = jnp.zeros_like(embed_scr)
        embed = embed_ref[...]
        high = embed.astype(BF16)
        rest = embed - high.astype(F32)
        middle = rest.astype(BF16)
        low = (rest - middle.astype(F32)).astype(BF16)
        for part, piece in enumerate((high, middle, low)):
            embed_scr[part * padded : part * padded + classes, :] = piece
        left_scr[...] = jnp.zeros_like(left_scr)
        for place in range(LANES // width):
            left_scr[place, place * width : (place + 1) * width, :] = left_ref[...]

    tokens = tokens_ref[pl.ds(step, 1), :]
    classes_iota = lax.broadcasted_iota(jnp.int32, (padded, residues), 0)
    onehot = (classes_iota == tokens).astype(F32).astype(BF16)
    onehot = jnp.concatenate([onehot, onehot, onehot], axis=0)
    initial = dot(onehot, embed_scr[...], ((0,), (0,))) + target_ref[...]
    normed = normalize(initial, gain_ref[...]).astype(BF16)
    query = (dot(normed, query_ref[...], ((1,), (0,))) * (1.0 / head_size**0.5)).astype(BF16)
    keys = dot(normed, key_ref[...], ((1,), (0,))).astype(BF16)
    values = dot(normed, value_ref[...], ((1,), (0,))).astype(BF16)
    place = lax.broadcasted_iota(jnp.int32, (1, LANES), 1) // head_size
    mixed = []
    for group in range(groups):
        lanes = slice(group * LANES, (group + 1) * LANES)
        for member in range(packed):
            mine = place == member
            rows = slice(member * residues, (member + 1) * residues)
            one_query = jnp.where(mine, query[:, lanes], jnp.zeros((), BF16))
            scores = dot(one_query, keys[:, lanes], ((1,), (1,))) + bias_scr[group * packed + member]
            expo = jnp.exp(scores - jnp.max(scores, axis=-1, keepdims=True))
            weights_scr[:, rows] = expo.astype(BF16)
            mixer_scr[rows, 0:LANES] = jnp.where(mine, values[:, lanes], jnp.zeros((), BF16))
            mixer_scr[rows, LANES:] = jnp.broadcast_to(
                jnp.where(mine, jnp.ones((), BF16), jnp.zeros((), BF16)), (residues, LANES)
            )
        both = dot(weights_scr[...], mixer_scr[...], ((1,), (0,)))
        mixed.append(both[:, :LANES] / both[:, LANES:])
    gate = jax.nn.sigmoid(dot(normed, gate_ref[...], ((1,), (0,))) + gate_bias_ref[...])
    mixed = (jnp.concatenate(mixed, axis=1) * gate).astype(BF16)
    updated = initial + dot(mixed, output_ref[...], ((1,), (0,)))
    updated_ref[0] = updated
    normed_two = normalize(updated, gain_two_ref[...])
    normed_scr[:, pl.ds(step, 1), :] = normed_two[:, None, :]
    factor_scr[:, pl.ds(step, 1), :] = dot(
        right_ref[...], normed_two.astype(BF16), ((1,), (1,))
    )[:, None, :]

    @pl.when(step == pl.num_programs(0) - 1)
    def finish():
        right = factor_scr[...].astype(BF16)
        by_owner = normed_scr.reshape(owners, owned, sequences, features)
        count = LANES // width
        for quarter in range(owned // count):
            total = jnp.zeros((owners * sequences, LANES), F32)
            for place in range(count):
                rows = by_owner[:, quarter * count + place].reshape(owners * sequences, features)
                total += dot(rows.astype(BF16), left_scr[place], ((1,), (1,)))
            slab, lane = divmod(quarter * LANES, residues)
            owner_scr[:, slab, :, lane : lane + LANES] = total.astype(BF16).reshape(owners, sequences, LANES)
        mine = lax.axis_index("wide") // inner
        for shift, message_ref in enumerate(message_refs):
            target = lax.rem(mine + shift, outer) * inner
            message_ref[0:width] = right
            message_ref[width:] = owner_scr[pl.ds(target, inner)].reshape(inner * slabs, sequences, residues)


def attention(
    tokens,
    offsets,
    target,
    embed,
    gain,
    query_weight,
    key_weight,
    value_weight,
    gate_weight,
    gate_bias,
    output_weight,
    relative,
    gain_two,
    left_weight,
    right_weight,
    owners,
    outer,
):
    sequences, residues = tokens.shape
    features = target.shape[1]
    heads = relative.shape[1]
    head_size = query_weight.shape[1] // heads
    packed = LANES // head_size
    width = left_weight.shape[1]
    owned = residues // owners
    slabs = owned * width // residues
    padded = -(-embed.shape[0] // 32) * 32
    operands = (
        tokens,
        offsets.reshape(1, -1),
        target,
        embed,
        gain.reshape(1, -1),
        query_weight,
        key_weight,
        value_weight,
        gate_weight,
        gate_bias.reshape(1, -1),
        output_weight,
        relative.T,
        gain_two.reshape(1, -1),
        left_weight.T,
        right_weight.T,
    )
    whole = lambda x: pl.BlockSpec(x.shape, lambda s, n=x.ndim: (0,) * n)
    message = (width + owners // outer * slabs, sequences, residues)
    outs = (jax.ShapeDtypeStruct((sequences, residues, features), F32),) + (
        jax.ShapeDtypeStruct(message, BF16),
    ) * outer
    return pl.pallas_call(
        functools.partial(attention_kernel, heads, owners, outer),
        grid=(sequences,),
        in_specs=[whole(x) for x in operands],
        out_specs=(pl.BlockSpec((1, residues, features), lambda s: (s, 0, 0)),)
        + tuple(whole(x) for x in outs[1:]),
        out_shape=outs,
        scratch_shapes=[
            pltpu.VMEM((heads, residues, residues), F32),
            pltpu.VMEM((LANES, LANES), F32),
            pltpu.VMEM((3 * padded, features), BF16),
            pltpu.VMEM((LANES // width, LANES, features), BF16),
            pltpu.VMEM((residues, packed * residues), BF16),
            pltpu.VMEM((packed * residues, 2 * LANES), BF16),
            pltpu.VMEM((residues, sequences, features), F32),
            pltpu.VMEM((width, sequences, residues), F32),
            pltpu.VMEM((owners, slabs, sequences, residues), BF16),
        ],
        name="attention",
    )(*operands)


def spread(messages, devices):
    outer = len(messages)
    inner = devices // outer
    core = 2 if inner % 2 == 0 else 1

    def move(piece, target):
        return lax.ppermute(piece, "wide", [(d, target(d)) for d in range(devices)])

    pieces = [messages[0]] + [
        move(message, lambda d, k=shift: (d // inner + k) % outer * inner + d % inner)
        for shift, message in enumerate(messages)
        if shift
    ]
    for axis, stride in ((inner // core, core), (core, 1)):
        pieces = pieces + [
            move(piece, lambda d, k=shift: d + ((d // stride + k) % axis - d // stride % axis) * stride)
            for shift in range(1, axis)
            for piece in pieces
        ]
    return pieces


def pair_kernel(devices, inner, weight_ref, bias_ref, *rest_refs):
    piece_refs = rest_refs[:devices]
    out_ref, right_scr, left_scr, flat_scr, outer_scr, weight_scr, wide_scr, sems = rest_refs[devices:]
    width, total, residues = right_scr.shape
    slabs = left_scr.shape[0]
    sequences = total // devices
    block = out_ref.shape[0]

    @pl.when(pl.program_id(0) == 0)
    def prepare():
        mine = lax.rem(lax.axis_index("wide"), inner) * slabs + width
        copies = []
        for number, piece_ref in enumerate(piece_refs):
            rows = pl.ds(number * sequences, sequences)
            copies.append(
                pltpu.make_async_copy(
                    piece_ref.at[pl.ds(mine, slabs)], left_scr.at[:, rows], sems.at[0, number]
                )
            )
            copies.append(
                pltpu.make_async_copy(
                    piece_ref.at[pl.ds(0, width)], right_scr.at[:, rows], sems.at[1, number]
                )
            )
        for copy in copies:
            copy.start()
        wide_scr[...] = weight_ref[...].astype(F32)
        for e in range(width):
            piece = wide_scr[pl.ds(e, width, stride=width), :]
            weight_scr[:, e * width : (e + 1) * width] = piece.T.astype(BF16)
        for copy in copies:
            copy.wait()
        for slab in range(slabs):
            flat_scr[slab * residues : (slab + 1) * residues, :] = left_scr[slab].astype(F32).T.astype(BF16)

    rows = block * width
    left = flat_scr[pl.ds(pl.multiple_of(pl.program_id(0) * rows, rows), rows), :]
    for e in range(width):
        product = dot(left, right_scr[e], ((1,), (0,))).astype(BF16)
        outer_scr[:, e * width : (e + 1) * width, :] = product.reshape(block, width, residues)
    for i in range(block):
        projected = dot(weight_scr[...], outer_scr[i], ((1,), (0,)))
        out_ref[i] = projected.T * (1.0 / total) + bias_ref[...]


def pair_features(pieces, weight, bias, inner, blocks):
    devices = len(pieces)
    _, sequences, residues = pieces[0].shape
    total = sequences * devices
    channels = weight.shape[1]
    width = round(weight.shape[0] ** 0.5)
    owned = residues // devices
    block = owned // blocks
    slabs = owned * width // residues
    return pl.pallas_call(
        functools.partial(pair_kernel, devices, inner),
        grid=(blocks,),
        in_specs=[
            pl.BlockSpec(weight.shape, lambda i: (0, 0)),
            pl.BlockSpec((1, channels), lambda i: (0, 0)),
        ]
        + [pl.BlockSpec(memory_space=pl.ANY)] * devices,
        out_specs=pl.BlockSpec((block, residues, channels), lambda i: (i, 0, 0)),
        out_shape=jax.ShapeDtypeStruct((owned, residues, channels), F32),
        scratch_shapes=[
            pltpu.VMEM((width, total, residues), BF16),
            pltpu.VMEM((slabs, total, residues), BF16),
            pltpu.VMEM((owned * width, total), BF16),
            pltpu.VMEM((block, width * width, residues), BF16),
            pltpu.VMEM((channels, width * width), BF16),
            pltpu.VMEM(weight.shape, F32),
            pltpu.SemaphoreType.DMA((2, devices)),
        ],
        name="pair",
    )(weight, bias.reshape(1, -1), *pieces)


def shards(
    alignment_token_ids,
    residue_index_offsets,
    target_residue_feature,
    token_embedding_table,
    attention_norm_gain,
    query_weight,
    key_weight,
    value_weight,
    gate_weight,
    gate_offset_bias,
    output_weight,
    relative_position_table,
    product_norm_gain,
    left_weight,
    right_weight,
    pair_weight,
    pair_projection_bias,
):
    devices = lax.axis_size("wide")
    core = 2 if devices % 2 == 0 else 1
    inner = 2 * core if devices % (2 * core) == 0 else core
    updated, *messages = attention(
        alignment_token_ids,
        residue_index_offsets,
        target_residue_feature,
        token_embedding_table,
        attention_norm_gain,
        query_weight,
        key_weight,
        value_weight,
        gate_weight,
        gate_offset_bias,
        output_weight,
        relative_position_table,
        product_norm_gain,
        left_weight,
        right_weight,
        devices,
        devices // inner,
    )
    pieces = spread(messages, devices)
    pair = pair_features(pieces, pair_weight, pair_projection_bias, inner, 2)
    return (updated, pair)


def solution(mesh):
    placed = (P(("groups", "wide"), None), P("groups"), P("groups", None)) + (P(),) * 14
    return jax.shard_map(
        shards,
        mesh=mesh,
        in_specs=placed,
        out_specs=(P(("groups", "wide"), None, None), P(("groups", "wide"), None, None)),
        check_vma=False,
    )
```

```python
import functools
import math

import jax
import jax.numpy as jnp
from jax import lax
from jax.experimental import pallas as pl
from jax.experimental.pallas import tpu as pltpu
from jax.sharding import PartitionSpec as P

REACH = 32
LANES = 128
F32 = jnp.float32
BF16 = jnp.bfloat16


def dot(a, b, axes):
    return lax.dot_general(a, b, (axes, ((), ())), preferred_element_type=F32)


def normalize(values, gain):
    center = jnp.mean(values, axis=-1, keepdims=True)
    centred = values - center
    spread = jnp.mean(centred * centred, axis=-1, keepdims=True)
    return centred * lax.rsqrt(spread + 1e-05) * gain


def room(shapes):
    total = 0
    for shape, dtype in shapes:
        total += math.prod(shape) * jnp.dtype(dtype).itemsize
    return total


def attention_kernel(heads, owners, outer, first, together, aliased, *refs):
    (
        tokens_ref,
        offsets_ref,
        target_ref,
        embed_ref,
        gain_ref,
        query_ref,
        key_ref,
        value_ref,
        gate_ref,
        gate_bias_ref,
        output_ref,
        relative_ref,
        gain_two_ref,
        left_ref,
        right_ref,
    ) = refs[:15]
    updated_ref, *rest_refs = refs[15 + aliased :]
    message_refs = rest_refs[:outer]
    (
        bias_scr,
        relative_scr,
        embed_scr,
        left_scr,
        weights_scr,
        mixer_scr,
        normed_scr,
        factor_scr,
        owner_scr,
    ) = rest_refs[outer:]
    step = pl.program_id(0)
    residues, features = target_ref.shape
    head_size = query_ref.shape[1] // heads
    packed = LANES // head_size
    groups = heads // packed
    classes = embed_ref.shape[0]
    padded = embed_scr.shape[0] // 3
    width = left_ref.shape[0]
    bins = relative_ref.shape[1]
    inner = owners // outer
    owned = residues // owners
    count = factor_scr.shape[1] // width
    halves = owner_scr.shape[1] // count
    reach = owned // halves
    span = residues // reach * count

    @pl.when(step == 0)
    def prepare():
        relative_scr[...] = jnp.zeros_like(relative_scr)
        relative_scr[0:heads, 0:bins] = relative_ref[...]
        table = relative_scr[...]
        row = offsets_ref[...]
        column = jnp.broadcast_to(row, (LANES, residues)).T
        for block in range(residues // LANES):
            lanes = slice(block * LANES, (block + 1) * LANES)
            index = jnp.clip(row[:, lanes] - column, -REACH, REACH) + REACH
            for head in range(heads):
                source = jnp.broadcast_to(table[head : head + 1, :], (residues, LANES))
                bias_scr[head, :, lanes] = jnp.take_along_axis(source, index, axis=1)
        embed_scr[...] = jnp.zeros_like(embed_scr)
        embed = embed_ref[...]
        high = embed.astype(BF16)
        rest = embed - high.astype(F32)
        middle = rest.astype(BF16)
        low = (rest - middle.astype(F32)).astype(BF16)
        for part, piece in enumerate((high, middle, low)):
            embed_scr[part * padded : part * padded + classes, :] = piece
        left_scr[...] = jnp.zeros_like(left_scr)
        for place in range(LANES // width):
            left_scr[place, place * width : (place + 1) * width, :] = left_ref[...]
        place = lax.broadcasted_iota(jnp.int32, (1, LANES), 1) // head_size
        for member in range(packed):
            ones = jnp.where(place == member, jnp.ones((), BF16), jnp.zeros((), BF16))
            for k in range(together):
                mixer_scr[k, member * residues : (member + 1) * residues, LANES:] = jnp.broadcast_to(
                    ones, (residues, LANES)
                )

    place = lax.broadcasted_iota(jnp.int32, (1, LANES), 1) // head_size
    blank = jnp.zeros((), BF16)
    members = range(together)
    rows = [step * together + k for k in members]
    initial, normed, query, keys, values, gates = [], [], [], [], [], []
    classes_iota = lax.broadcasted_iota(jnp.int32, (padded, residues), 0)
    for k in members:
        tokens = tokens_ref[pl.ds(first + rows[k], 1), :]
        onehot = (classes_iota == tokens).astype(F32).astype(BF16)
        onehot = jnp.concatenate([onehot, onehot, onehot], axis=0)
        initial.append(dot(onehot, embed_scr[...], ((0,), (0,))) + target_ref[...])
    for k in members:
        normed.append(normalize(initial[k], gain_ref[...]).astype(BF16))
    for k in members:
        product = dot(normed[k], query_ref[...], ((1,), (0,)))
        query.append((product * (1.0 / head_size**0.5)).astype(BF16))
        keys.append(dot(normed[k], key_ref[...], ((1,), (0,))).astype(BF16))
        values.append(dot(normed[k], value_ref[...], ((1,), (0,))).astype(BF16))
    mixed = [[] for _ in members]
    for group in range(groups):
        lanes = slice(group * LANES, (group + 1) * LANES)
        for member in range(packed):
            mine = place == member
            columns = slice(member * residues, (member + 1) * residues)
            for k in members:
                one_query = jnp.where(mine, query[k][:, lanes], blank)
                scores = dot(one_query, keys[k][:, lanes], ((1,), (1,)))
                scores = scores + bias_scr[group * packed + member]
                expo = jnp.exp(scores - jnp.max(scores, axis=-1, keepdims=True))
                weights_scr[k, :, columns] = expo.astype(BF16)
                mixer_scr[k, columns, 0:LANES] = jnp.where(mine, values[k][:, lanes], blank)
        for k in members:
            both = dot(weights_scr[k], mixer_scr[k], ((1,), (0,)))
            mixed[k].append(both[:, :LANES] / both[:, LANES:])
    for k in members:
        gates.append(jax.nn.sigmoid(dot(normed[k], gate_ref[...], ((1,), (0,))) + gate_bias_ref[...]))
    for k in members:
        whole = (jnp.concatenate(mixed[k], axis=1) * gates[k]).astype(BF16)
        updated = initial[k] + dot(whole, output_ref[...], ((1,), (0,)))
        updated_ref[k] = updated
        normed_two = normalize(updated, gain_two_ref[...])
        for tile in range(features // LANES):
            lanes = slice(tile * LANES, (tile + 1) * LANES)
            for block in range(residues // reach):
                normed_scr[tile, pl.ds(block * count + rows[k], reach, stride=span), :] = normed_two[
                    block * reach : (block + 1) * reach, lanes
                ]
        right = dot(right_ref[...], normed_two.astype(BF16), ((1,), (1,)))
        for tile in range(residues // LANES):
            lanes = slice(tile * LANES, (tile + 1) * LANES)
            factor_scr[tile, pl.ds(rows[k], width, stride=count), :] = right[:, lanes]

    @pl.when(step == pl.num_programs(0) - 1)
    def finish():
        right = jnp.concatenate([factor_scr[t] for t in range(residues // LANES)], axis=1)
        right = right.astype(BF16).reshape(width // halves, halves * count, residues)
        fold = LANES // width
        for quarter in range(reach // fold):
            total = jnp.zeros((span, LANES), F32)
            for place in range(fold):
                start = (quarter * fold + place) * span
                for tile in range(features // LANES):
                    factors = normed_scr[tile, start : start + span, :].astype(BF16)
                    lanes = slice(tile * LANES, (tile + 1) * LANES)
                    total += dot(factors, left_scr[place, :, lanes], ((1,), (1,)))
            owner_scr[:, :, quarter * LANES : (quarter + 1) * LANES] = total.astype(BF16).reshape(
                owners, halves * count, LANES
            )
        spare = residues - reach * width
        if spare:
            owner_scr[:, :, reach * width :] = jnp.zeros((owners, halves * count, spare), BF16)
        mine = lax.axis_index("wide") // inner
        for shift, message_ref in enumerate(message_refs):
            target = lax.rem(mine + shift, outer) * inner
            message_ref[0 : width // halves] = right
            message_ref[width // halves :] = owner_scr[pl.ds(target, inner)]


def attention(operands, heads, owners, outer, part, parts, updated):
    tokens, _, target, embed, _, query_weight = operands[:6]
    left_weight = operands[13]
    sequences, residues = tokens.shape
    features = target.shape[1]
    head_size = query_weight.shape[1] // heads
    packed = LANES // head_size
    width = left_weight.shape[0]
    padded = -(-embed.shape[0] // 32) * 32
    count = sequences // parts
    halves = max(1, 8 // count)
    together = 2 if count % 2 == 0 else 1
    first = part * count
    whole = lambda x: pl.BlockSpec(x.shape, lambda s, n=x.ndim: (0,) * n)
    message = (width // halves + owners // outer, halves * count, residues)
    outs = (jax.ShapeDtypeStruct((sequences, residues, features), F32),) + (
        jax.ShapeDtypeStruct(message, BF16),
    ) * outer
    scratch = [
        ((heads, residues, residues), F32),
        ((heads, LANES), F32),
        ((3 * padded, features), BF16),
        ((LANES // width, LANES, features), BF16),
        ((together, residues, packed * residues), BF16),
        ((together, packed * residues, 2 * LANES), BF16),
        ((features // LANES, residues * count, LANES), F32),
        ((residues // LANES, width * count, LANES), F32),
        ((owners, halves * count, residues), BF16),
    ]
    used = room(scratch) + sum(2 * room([(x.shape, x.dtype)]) for x in operands)
    used += 2 * outer * room([(message, BF16)]) + 2 * room([((together, residues, features), F32)])
    in_specs = [whole(x) for x in operands]
    aliases = {}
    if updated is not None:
        aliases = {len(operands): 0}
        in_specs.append(pl.BlockSpec(memory_space=pl.ANY))
        operands = operands + (updated,)
    return pl.pallas_call(
        functools.partial(attention_kernel, heads, owners, outer, first, together, len(aliases)),
        grid=(count // together,),
        in_specs=in_specs,
        out_specs=(
            pl.BlockSpec(
                (together, residues, features), lambda s, offset=first // together: (s + offset, 0, 0)
            ),
        )
        + tuple(whole(x) for x in outs[1:]),
        out_shape=outs,
        scratch_shapes=[pltpu.VMEM(shape, dtype) for shape, dtype in scratch],
        input_output_aliases=aliases,
        compiler_params=pltpu.CompilerParams(vmem_limit_bytes=used + 12 * 2**20),
        cost_estimate=pl.CostEstimate(
            flops=count * residues * (8 * features * features + 8 * heads * residues * LANES),
            transcendentals=count * heads * residues * residues,
            bytes_accessed=4 * count * residues * features,
        ),
        name="attention",
    )(*operands)


def spread(messages, devices):
    outer = len(messages)
    inner = devices // outer
    core = 2 if inner % 2 == 0 else 1

    def move(piece, target):
        return lax.ppermute(piece, "wide", [(d, target(d)) for d in range(devices)])

    pieces = [messages[0]] + [
        move(message, lambda d, k=shift: (d // inner + k) % outer * inner + d % inner)
        for shift, message in enumerate(messages)
        if shift
    ]
    for axis, stride in ((inner // core, core), (core, 1)):
        pieces = pieces + [
            move(piece, lambda d, k=shift: d + ((d // stride + k) % axis - d // stride % axis) * stride)
            for shift in range(1, axis)
            for piece in pieces
        ]
    return pieces


def order_kernel(weight_ref, out_ref, wide_scr):
    width = round(weight_ref.shape[0] ** 0.5)
    wide_scr[...] = weight_ref[...].astype(F32)
    for e in range(width):
        out_ref[:, e * width : (e + 1) * width] = wide_scr[pl.ds(e, width, stride=width), :].T.astype(BF16)


def ordered(weight):
    shape = weight.shape[::-1]
    return pl.pallas_call(
        order_kernel,
        out_shape=jax.ShapeDtypeStruct(shape, BF16),
        scratch_shapes=[pltpu.VMEM(weight.shape, F32)],
        compiler_params=pltpu.CompilerParams(vmem_limit_bytes=8 * 2**20),
        cost_estimate=pl.CostEstimate(flops=0, transcendentals=0, bytes_accessed=4 * math.prod(shape)),
        name="order",
    )(weight)


def pair_kernel(count, halves, inner, weight_ref, bias_ref, *rest_refs):
    pieces = len(rest_refs) - 6
    piece_refs = rest_refs[:pieces]
    out_ref, right_scr, left_scr, flat_scr, outer_scr, sems = rest_refs[pieces:]
    groups, depth, residues = right_scr.shape
    height = halves * count
    width = groups * halves
    block = out_ref.shape[0]
    half = flat_scr.shape[1] // halves

    @pl.when(pl.program_id(0) == 0)
    def prepare():
        mine = lax.rem(lax.axis_index("wide"), inner) + groups
        copies = []
        for number, piece_ref in enumerate(piece_refs):
            rows = pl.ds(number * height, height)
            copies.append(pltpu.make_async_copy(piece_ref.at[mine], left_scr.at[rows], sems.at[0, number]))
            copies.append(
                pltpu.make_async_copy(
                    piece_ref.at[pl.ds(0, groups)], right_scr.at[:, rows], sems.at[1, number]
                )
            )
        for copy in copies:
            copy.start()
        for copy in copies[0::2]:
            copy.wait()
        left = left_scr[:, 0:half].astype(F32)
        member = lax.broadcasted_iota(jnp.int32, (depth, 1), 0) % height // count
        for e in range(halves):
            for h in range(halves):
                moved = left
                if e != h:
                    moved = pltpu.roll(left.reshape(pieces, height, half), (e - h) % halves * count, 1)
                    moved = moved.reshape(depth, half)
                moved = jnp.where(member == e, moved, 0.0)
                flat_scr[e, h * half : (h + 1) * half, :] = moved.T.astype(BF16)
        for copy in copies[1::2]:
            copy.wait()

    rows = block * width
    start = pl.multiple_of(pl.program_id(0) * rows, rows)
    for group in range(groups):
        for e in range(halves):
            product = dot(flat_scr[e, pl.ds(start, rows), :], right_scr[group], ((1,), (0,))).astype(BF16)
            place = (group * halves + e) * width
            outer_scr[:, place : place + width, :] = product.reshape(block, width, residues)
    total = float(pieces * count)
    for i in range(block):
        projected = dot(weight_ref[...], outer_scr[i], ((1,), (0,)))
        out_ref[i] = projected.T * (1.0 / total) + bias_ref[...]


def pair_features(pieces, weight, bias, count, inner, owned, blocks):
    slabs, height, residues = pieces[0].shape
    halves = height // count
    groups = slabs - inner
    width = groups * halves
    depth = len(pieces) * height
    channels = weight.shape[0]
    block = owned // blocks
    scratch = [
        ((groups, depth, residues), BF16),
        ((depth, residues), BF16),
        ((halves, owned * width, depth), BF16),
        ((block, width * width, residues), BF16),
    ]
    used = room(scratch) + 2 * room([(weight.shape, BF16), ((block, residues, channels), F32)])
    return pl.pallas_call(
        functools.partial(pair_kernel, count, halves, inner),
        grid=(blocks,),
        in_specs=[
            pl.BlockSpec(weight.shape, lambda i: (0, 0)),
            pl.BlockSpec((1, channels), lambda i: (0, 0)),
        ]
        + [pl.BlockSpec(memory_space=pl.ANY)] * len(pieces),
        out_specs=pl.BlockSpec((block, residues, channels), lambda i: (i, 0, 0)),
        out_shape=jax.ShapeDtypeStruct((owned, residues, channels), F32),
        scratch_shapes=[pltpu.VMEM(shape, dtype) for shape, dtype in scratch]
        + [pltpu.SemaphoreType.DMA((2, len(pieces)))],
        compiler_params=pltpu.CompilerParams(vmem_limit_bytes=used + 12 * 2**20),
        name="pair",
    )(weight, bias.reshape(1, -1), *pieces)


def shards(
    alignment_token_ids,
    residue_index_offsets,
    target_residue_feature,
    token_embedding_table,
    attention_norm_gain,
    query_weight,
    key_weight,
    value_weight,
    gate_weight,
    gate_offset_bias,
    output_weight,
    relative_position_table,
    product_norm_gain,
    left_weight,
    right_weight,
    pair_weight,
    pair_projection_bias,
):
    devices = lax.axis_size("wide")
    core = 2 if devices % 2 == 0 else 1
    inner = 2 * core if devices % (2 * core) == 0 else core
    sequences, residues = alignment_token_ids.shape
    parts = 2 if sequences % 2 == 0 else 1
    operands = (
        alignment_token_ids,
        residue_index_offsets.reshape(1, -1),
        target_residue_feature,
        token_embedding_table,
        attention_norm_gain.reshape(1, -1),
        query_weight,
        key_weight,
        value_weight,
        gate_weight,
        gate_offset_bias.reshape(1, -1),
        output_weight,
        relative_position_table.T,
        product_norm_gain.reshape(1, -1),
        left_weight.T,
        right_weight.T,
    )
    heads = relative_position_table.shape[1]
    updated = None
    pieces = []
    for part in range(parts):
        updated, *messages = attention(operands, heads, devices, devices // inner, part, parts, updated)
        pieces += spread(messages, devices)
    pair = pair_features(
        pieces,
        ordered(pair_weight),
        pair_projection_bias,
        sequences // parts,
        inner,
        residues // devices,
        2,
    )
    return (updated, pair)


def solution(mesh):
    placed = (P(("groups", "wide"), None), P("groups"), P("groups", None)) + (P(),) * 14
    return jax.shard_map(
        shards,
        mesh=mesh,
        in_specs=placed,
        out_specs=(P(("groups", "wide"), None, None), P(("groups", "wide"), None, None)),
        check_vma=False,
    )
```

```python
import functools
import math

import jax
import jax.numpy as jnp
from jax import lax
from jax.experimental import pallas as pl
from jax.experimental.pallas import tpu as pltpu
from jax.sharding import PartitionSpec as P

REACH = 32
LANES = 128
F32 = jnp.float32
BF16 = jnp.bfloat16


def dot(a, b, axes):
    return lax.dot_general(a, b, (axes, ((), ())), preferred_element_type=F32)


def normalize(values, gain):
    center = jnp.mean(values, axis=-1, keepdims=True)
    centred = values - center
    spread = jnp.mean(centred * centred, axis=-1, keepdims=True)
    return centred * lax.rsqrt(spread + 1e-05) * gain


def meet(place, shift, size):
    if size & (size - 1):
        return (place + shift) % size
    return place ^ shift


def room(shapes):
    total = 0
    for shape, dtype in shapes:
        total += math.prod(shape) * jnp.dtype(dtype).itemsize
    return total


def attention_kernel(heads, owners, outer, together, *refs):
    (
        tokens_ref,
        offsets_ref,
        target_ref,
        embed_ref,
        gain_ref,
        query_ref,
        key_ref,
        value_ref,
        gate_ref,
        gate_bias_ref,
        output_ref,
        relative_ref,
        gain_two_ref,
        left_ref,
        right_ref,
    ) = refs[:15]
    updated_ref, *rest_refs = refs[15:]
    message_refs = rest_refs[:outer]
    (
        bias_scr,
        relative_scr,
        embed_scr,
        left_scr,
        weights_scr,
        mixer_scr,
        factor_scr,
        owner_scr,
        gather_scr,
    ) = rest_refs[outer:]
    step = pl.program_id(0)
    residues, features = target_ref.shape
    head_size = query_ref.shape[1] // heads
    packed = LANES // head_size
    groups = heads // packed
    classes = embed_ref.shape[0]
    padded = embed_scr.shape[0] // 3
    width = right_ref.shape[0]
    bins = relative_ref.shape[1]
    inner = owners // outer
    owned = residues // owners
    count = factor_scr.shape[1] // width
    slabs = owned * width // residues

    @pl.when(step == 0)
    def prepare():
        relative_scr[...] = jnp.zeros_like(relative_scr)
        relative_scr[0:heads, 0:bins] = relative_ref[...]
        table = relative_scr[...]
        row = offsets_ref[...]
        column = jnp.broadcast_to(row, (LANES, residues)).T
        for block in range(residues // LANES):
            lanes = slice(block * LANES, (block + 1) * LANES)
            start, stop = block * LANES, (block + 1) * LANES
            low = max(0, (start - REACH + 1) // 8 * 8)
            high = min(residues, -(-(stop + REACH) // 8) * 8)
            index = jnp.clip(row[:, lanes] - column[low:high], -REACH, REACH) + REACH
            for head in range(heads):
                source = jnp.broadcast_to(table[head : head + 1, :], (high - low, LANES))
                bias_scr[head, low:high, lanes] = jnp.take_along_axis(source, index, axis=1)
                if low:
                    after = table[head : head + 1, 2 * REACH : 2 * REACH + 1]
                    bias_scr[head, 0:low, lanes] = jnp.broadcast_to(after, (low, LANES))
                if high < residues:
                    before = table[head : head + 1, 0:1]
                    bias_scr[head, high:, lanes] = jnp.broadcast_to(before, (residues - high, LANES))
        embed_scr[...] = jnp.zeros_like(embed_scr)
        embed = embed_ref[...]
        high = embed.astype(BF16)
        rest = embed - high.astype(F32)
        middle = rest.astype(BF16)
        low = (rest - middle.astype(F32)).astype(BF16)
        for part, piece in enumerate((high, middle, low)):
            embed_scr[part * padded : part * padded + classes, :] = piece
        for tile in range(owned):
            left_scr[tile * width : (tile + 1) * width, :] = left_ref[...]
        gather_scr[...] = (
            lax.broadcasted_iota(jnp.int32, gather_scr.shape, 0)
            == lax.broadcasted_iota(jnp.int32, gather_scr.shape, 1) // owned
        ).astype(F32).astype(BF16)
        place = lax.broadcasted_iota(jnp.int32, (1, LANES), 1) // head_size
        for member in range(packed):
            ones = jnp.where(place == member, jnp.ones((), BF16), jnp.zeros((), BF16))
            for k in range(together):
                mixer_scr[k, member * residues : (member + 1) * residues, LANES:] = jnp.broadcast_to(
                    ones, (residues, LANES)
                )

    place = lax.broadcasted_iota(jnp.int32, (1, LANES), 1) // head_size
    blank = jnp.zeros((), BF16)
    members = range(together)
    diagonal = (
        lax.broadcasted_iota(jnp.int32, (residues, owned * width), 0) % owned
        == lax.broadcasted_iota(jnp.int32, (residues, owned * width), 1) // width
    )
    rows = [step * together + k for k in members]
    initial, normed, query, keys, values, gates = [], [], [], [], [], []
    classes_iota = lax.broadcasted_iota(jnp.int32, (padded, residues), 0)
    for k in members:
        tokens = tokens_ref[pl.ds(rows[k], 1), :]
        onehot = (classes_iota == tokens).astype(F32).astype(BF16)
        onehot = jnp.concatenate([onehot, onehot, onehot], axis=0)
        initial.append(dot(onehot, embed_scr[...], ((0,), (0,))) + target_ref[...])
    for k in members:
        normed.append(normalize(initial[k], gain_ref[...]).astype(BF16))
    for k in members:
        product = dot(normed[k], query_ref[...], ((1,), (0,)))
        query.append((product * (1.0 / head_size**0.5)).astype(BF16))
        keys.append(dot(normed[k], key_ref[...], ((1,), (0,))).astype(BF16))
        values.append(dot(normed[k], value_ref[...], ((1,), (0,))).astype(BF16))
    mixed = [[] for _ in members]
    for group in range(groups):
        lanes = slice(group * LANES, (group + 1) * LANES)
        for member in range(packed):
            mine = place == member
            columns = slice(member * residues, (member + 1) * residues)
            for k in members:
                one_query = jnp.where(mine, query[k][:, lanes], blank)
                scores = dot(one_query, keys[k][:, lanes], ((1,), (1,)))
                scores = scores + bias_scr[group * packed + member]
                expo = jnp.exp(scores - jnp.max(scores, axis=-1, keepdims=True))
                weights_scr[k, :, columns] = expo.astype(BF16)
                mixer_scr[k, columns, 0:LANES] = jnp.where(mine, values[k][:, lanes], blank)
        for k in members:
            both = dot(weights_scr[k], mixer_scr[k], ((1,), (0,)))
            mixed[k].append(both[:, :LANES] / both[:, LANES:])
    for k in members:
        gates.append(jax.nn.sigmoid(dot(normed[k], gate_ref[...], ((1,), (0,))) + gate_bias_ref[...]))
    for k in members:
        whole = (jnp.concatenate(mixed[k], axis=1) * gates[k]).astype(BF16)
        updated = initial[k] + dot(whole, output_ref[...], ((1,), (0,)))
        updated_ref[k] = updated
        normed_two = normalize(updated, gain_two_ref[...])
        narrow = normed_two.astype(BF16)
        spread_left = dot(narrow, left_scr[...], ((1,), (1,)))
        spread_left = jnp.where(diagonal, spread_left, 0.0).astype(BF16)
        folded = dot(gather_scr[...], spread_left, ((1,), (0,)))
        for tile in range(owned * width // LANES):
            lanes = slice(tile * LANES, (tile + 1) * LANES)
            owner_scr[tile, pl.ds(rows[k], owners, stride=count), :] = folded[:, lanes]
        right = dot(right_ref[...], narrow, ((1,), (1,)))
        for tile in range(residues // LANES):
            lanes = slice(tile * LANES, (tile + 1) * LANES)
            factor_scr[tile, pl.ds(rows[k], width, stride=count), :] = right[:, lanes]

    @pl.when(step == pl.num_programs(0) - 1)
    def finish():
        right = jnp.concatenate([factor_scr[t] for t in range(residues // LANES)], axis=1)
        right = right.astype(BF16).reshape(width, count, residues)
        mine = lax.axis_index("wide") // inner
        per = residues // LANES
        for shift, message_ref in enumerate(message_refs):
            target = meet(mine, shift, outer) * inner
            message_ref[0:width] = right
            for k in range(inner):
                start = pl.multiple_of((target + k) * count, count)
                for slab in range(slabs):
                    block = [owner_scr[slab * per + t, pl.ds(start, count), :] for t in range(per)]
                    message_ref[width + k * slabs + slab] = jnp.concatenate(block, axis=1).astype(BF16)


def attention(operands, heads, owners, outer):
    tokens, _, target, embed, _, query_weight = operands[:6]
    left_weight, right_weight = operands[13:15]
    count, residues = tokens.shape
    features = target.shape[1]
    head_size = query_weight.shape[1] // heads
    packed = LANES // head_size
    width = right_weight.shape[0]
    owned = residues // owners
    padded = -(-embed.shape[0] // 32) * 32
    together = 2 if count % 2 == 0 else 1
    whole = lambda x: pl.BlockSpec(x.shape, lambda s, n=x.ndim: (0,) * n)
    slabs = owned * width // residues
    message = (width + owners // outer * slabs, count, residues)
    outs = (jax.ShapeDtypeStruct((count, residues, features), F32),) + (
        jax.ShapeDtypeStruct(message, BF16),
    ) * outer
    scratch = [
        ((heads, residues, residues), F32),
        ((heads, LANES), F32),
        ((3 * padded, features), BF16),
        ((owned * width, features), BF16),
        ((together, residues, packed * residues), BF16),
        ((together, packed * residues, 2 * LANES), BF16),
        ((residues // LANES, width * count, LANES), F32),
        ((owned * width // LANES, owners * count, LANES), F32),
        ((owners, residues), BF16),
    ]
    return pl.pallas_call(
        functools.partial(attention_kernel, heads, owners, outer, together),
        grid=(count // together,),
        in_specs=[whole(x) for x in operands],
        out_specs=(pl.BlockSpec((together, residues, features), lambda s: (s, 0, 0)),)
        + tuple(whole(x) for x in outs[1:]),
        out_shape=outs,
        scratch_shapes=[pltpu.VMEM(shape, dtype) for shape, dtype in scratch],
        cost_estimate=pl.CostEstimate(
            flops=count * residues * (8 * features * features + 8 * heads * residues * LANES),
            transcendentals=count * heads * residues * residues,
            bytes_accessed=4 * count * residues * features,
        ),
        name="attention",
    )(*operands)


def spread(messages, devices, weight):
    outer = len(messages)
    inner = devices // outer
    core = 2 if inner % 2 == 0 else 1

    def move(piece, target):
        return lax.ppermute(piece, "wide", [(d, target(d)) for d in range(devices)])

    pieces = [messages[0]] + [
        move(message, lambda d, k=shift: meet(d // inner, k, outer) * inner + d % inner)
        for shift, message in enumerate(messages)
        if shift
    ]
    if outer > 1:
        pieces[1], weight = lax.optimization_barrier((pieces[1], weight))
    for axis, stride in ((inner // core, core), (core, 1)):
        pieces = pieces + [
            move(piece, lambda d, k=shift: d + ((d // stride + k) % axis - d // stride % axis) * stride)
            for shift in range(1, axis)
            for piece in pieces
        ]
    return pieces, weight


def order_kernel(weight_ref, out_ref, wide_scr):
    width = round(weight_ref.shape[0] ** 0.5)
    wide_scr[...] = weight_ref[...].astype(F32)
    for e in range(width):
        out_ref[:, e * width : (e + 1) * width] = wide_scr[pl.ds(e, width, stride=width), :].T.astype(BF16)


def ordered(weight):
    shape = weight.shape[::-1]
    return pl.pallas_call(
        order_kernel,
        out_shape=jax.ShapeDtypeStruct(shape, BF16),
        scratch_shapes=[pltpu.VMEM(weight.shape, F32)],
        compiler_params=pltpu.CompilerParams(vmem_limit_bytes=8 * 2**20),
        cost_estimate=pl.CostEstimate(flops=0, transcendentals=0, bytes_accessed=4 * math.prod(shape)),
        name="order",
    )(weight)


def pair_kernel(count, halves, inner, weight_ref, bias_ref, *rest_refs):
    pieces = len(rest_refs) - 6
    piece_refs = rest_refs[:pieces]
    out_ref, right_scr, left_scr, flat_scr, outer_scr, sems = rest_refs[pieces:]
    groups, depth, residues = right_scr.shape
    height = halves * count
    width = groups * halves
    block = out_ref.shape[0]
    half = flat_scr.shape[1] // halves
    slabs = left_scr.shape[0]

    @pl.when(pl.program_id(0) == 0)
    def prepare():
        mine = lax.rem(lax.axis_index("wide"), inner) * slabs + groups
        copies = []
        for number, piece_ref in enumerate(piece_refs):
            rows = pl.ds(number * height, height)
            copies.append(
                pltpu.make_async_copy(
                    piece_ref.at[pl.ds(mine, slabs)], left_scr.at[:, rows], sems.at[0, number]
                )
            )
            copies.append(
                pltpu.make_async_copy(
                    piece_ref.at[pl.ds(0, groups)], right_scr.at[:, rows], sems.at[1, number]
                )
            )
        for copy in copies:
            copy.start()
        for copy in copies[0::2]:
            copy.wait()
        left = jnp.concatenate([left_scr[slab] for slab in range(slabs)], axis=1)[:, 0:half].astype(F32)
        member = lax.broadcasted_iota(jnp.int32, (depth, 1), 0) % height // count
        for e in range(halves):
            for h in range(halves):
                moved = left
                if e != h:
                    moved = pltpu.roll(left.reshape(pieces, height, half), (e - h) % halves * count, 1)
                    moved = moved.reshape(depth, half)
                moved = jnp.where(member == e, moved, 0.0)
                flat_scr[e, h * half : (h + 1) * half, :] = moved.T.astype(BF16)
        for copy in copies[1::2]:
            copy.wait()

    rows = block * width
    start = pl.multiple_of(pl.program_id(0) * rows, rows)
    for group in range(groups):
        for e in range(halves):
            product = dot(flat_scr[e, pl.ds(start, rows), :], right_scr[group], ((1,), (0,))).astype(BF16)
            place = (group * halves + e) * width
            outer_scr[:, place : place + width, :] = product.reshape(block, width, residues)
    total = float(pieces * count)
    for i in range(block):
        projected = dot(weight_ref[...], outer_scr[i], ((1,), (0,)))
        out_ref[i] = projected.T * (1.0 / total) + bias_ref[...]


def pair_features(pieces, weight, bias, count, inner, owned, blocks):
    slabs, height, residues = pieces[0].shape
    halves = height // count
    width = round(weight.shape[1] ** 0.5)
    groups = width // halves
    slabs = (slabs - groups) // inner
    depth = len(pieces) * height
    channels = weight.shape[0]
    block = owned // blocks
    scratch = [
        ((groups, depth, residues), BF16),
        ((slabs, depth, residues), BF16),
        ((halves, owned * width, depth), BF16),
        ((block, width * width, residues), BF16),
    ]
    used = room(scratch) + 2 * room([(weight.shape, BF16), ((block, residues, channels), F32)])
    return pl.pallas_call(
        functools.partial(pair_kernel, count, halves, inner),
        grid=(blocks,),
        in_specs=[
            pl.BlockSpec(weight.shape, lambda i: (0, 0)),
            pl.BlockSpec((1, channels), lambda i: (0, 0)),
        ]
        + [pl.BlockSpec(memory_space=pl.ANY)] * len(pieces),
        out_specs=pl.BlockSpec((block, residues, channels), lambda i: (i, 0, 0)),
        out_shape=jax.ShapeDtypeStruct((owned, residues, channels), F32),
        scratch_shapes=[pltpu.VMEM(shape, dtype) for shape, dtype in scratch]
        + [pltpu.SemaphoreType.DMA((2, len(pieces)))],
        compiler_params=pltpu.CompilerParams(vmem_limit_bytes=used + 12 * 2**20),
        name="pair",
    )(weight, bias.reshape(1, -1), *pieces)


def shards(
    alignment_token_ids,
    residue_index_offsets,
    target_residue_feature,
    token_embedding_table,
    attention_norm_gain,
    query_weight,
    key_weight,
    value_weight,
    gate_weight,
    gate_offset_bias,
    output_weight,
    relative_position_table,
    product_norm_gain,
    left_weight,
    right_weight,
    pair_weight,
    pair_projection_bias,
):
    devices = lax.axis_size("wide")
    core = 2 if devices % 2 == 0 else 1
    inner = 2 * core if devices % (2 * core) == 0 else core
    sequences, residues = alignment_token_ids.shape
    operands = (
        alignment_token_ids,
        residue_index_offsets.reshape(1, -1),
        target_residue_feature,
        token_embedding_table,
        attention_norm_gain.reshape(1, -1),
        query_weight,
        key_weight,
        value_weight,
        gate_weight,
        gate_offset_bias.reshape(1, -1),
        output_weight,
        relative_position_table.T,
        product_norm_gain.reshape(1, -1),
        left_weight.T,
        right_weight.T,
    )
    heads = relative_position_table.shape[1]
    updated, *messages = attention(operands, heads, devices, devices // inner)
    pieces, weight = spread(messages, devices, ordered(pair_weight))
    pair = pair_features(
        pieces,
        weight,
        pair_projection_bias,
        sequences,
        inner,
        residues // devices,
        2,
    )
    return (updated, pair)


def solution(mesh):
    placed = (P(("groups", "wide"), None), P("groups"), P("groups", None)) + (P(),) * 14
    return jax.shard_map(
        shards,
        mesh=mesh,
        in_specs=placed,
        out_specs=(P(("groups", "wide"), None, None), P(("groups", "wide"), None, None)),
        check_vma=False,
    )
```

```python
import functools
import math

import jax
import jax.numpy as jnp
from jax import lax
from jax.experimental import pallas as pl
from jax.experimental.pallas import tpu as pltpu
from jax.sharding import PartitionSpec as P


REACH = 32
LANES = 128
F32 = jnp.float32
BF16 = jnp.bfloat16


def dot(a, b, axes):
    return lax.dot_general(a, b, (axes, ((), ())), preferred_element_type=F32)


def normalize(values, gain):
    center = jnp.mean(values, axis=-1, keepdims=True)
    centred = values - center
    spread = jnp.mean(centred * centred, axis=-1, keepdims=True)
    return centred * lax.rsqrt(spread + 1e-05) * gain


def meet(place, shift, size):
    if size & (size - 1):
        return (place + shift) % size
    return place ^ shift


def nearest(devices):
    core = 2 if devices % 2 == 0 else 1
    return 2 * core if devices % (2 * core) == 0 else core


def room(shapes):
    total = 0
    for shape, dtype in shapes:
        total += math.prod(shape) * jnp.dtype(dtype).itemsize
    return total


def attention_kernel(heads, owners, outer, together, *refs):
    (
        tokens_ref,
        offsets_ref,
        target_ref,
        embed_ref,
        gain_ref,
        query_ref,
        key_ref,
        value_ref,
        gate_ref,
        gate_bias_ref,
        output_ref,
        relative_ref,
        gain_two_ref,
        left_ref,
        right_ref,
    ) = refs[:15]
    updated_ref, *rest_refs = refs[15:]
    message_refs = rest_refs[:outer]
    (
        bias_scr,
        relative_scr,
        embed_scr,
        left_scr,
        weights_scr,
        mixer_scr,
        factor_scr,
        owner_scr,
        gather_scr,
    ) = rest_refs[outer:]
    step = pl.program_id(0)
    residues, _ = target_ref.shape
    head_size = query_ref.shape[1] // heads
    packed = LANES // head_size
    groups = heads // packed
    classes = embed_ref.shape[0]
    padded = embed_scr.shape[0] // 3
    width = right_ref.shape[0]
    bins = relative_ref.shape[1]
    inner = owners // outer
    owned = residues // owners
    count = factor_scr.shape[1] // width
    slabs = owned * width // residues

    @pl.when(step == 0)
    def prepare():
        relative_scr[...] = jnp.zeros_like(relative_scr)
        relative_scr[0:heads, 0:bins] = relative_ref[...]
        table = relative_scr[...]
        row = offsets_ref[...]
        column = jnp.broadcast_to(row, (LANES, residues)).T
        for block in range(residues // LANES):
            lanes = slice(block * LANES, (block + 1) * LANES)
            start, stop = block * LANES, (block + 1) * LANES
            low = max(0, (start - REACH + 1) // 8 * 8)
            high = min(residues, -(-(stop + REACH) // 8) * 8)
            index = jnp.clip(row[:, lanes] - column[low:high], -REACH, REACH) + REACH
            for head in range(heads):
                source = jnp.broadcast_to(table[head : head + 1, :], (high - low, LANES))
                bias_scr[head, low:high, lanes] = jnp.take_along_axis(source, index, axis=1)
                if low:
                    after = table[head : head + 1, 2 * REACH : 2 * REACH + 1]
                    bias_scr[head, 0:low, lanes] = jnp.broadcast_to(after, (low, LANES))
                if high < residues:
                    before = table[head : head + 1, 0:1]
                    bias_scr[head, high:, lanes] = jnp.broadcast_to(before, (residues - high, LANES))
        embed_scr[...] = jnp.zeros_like(embed_scr)
        embed = embed_ref[...]
        high = embed.astype(BF16)
        rest = embed - high.astype(F32)
        middle = rest.astype(BF16)
        low = (rest - middle.astype(F32)).astype(BF16)
        for part, piece in enumerate((high, middle, low)):
            embed_scr[part * padded : part * padded + classes, :] = piece
        for tile in range(owned):
            left_scr[tile * width : (tile + 1) * width, :] = left_ref[...]
        gather_scr[...] = (
            lax.broadcasted_iota(jnp.int32, gather_scr.shape, 0)
            == lax.broadcasted_iota(jnp.int32, gather_scr.shape, 1) // owned
        ).astype(F32).astype(BF16)
        place = lax.broadcasted_iota(jnp.int32, (1, LANES), 1) // head_size
        for member in range(packed):
            ones = jnp.where(place == member, jnp.ones((), BF16), jnp.zeros((), BF16))
            for k in range(together):
                mixer_scr[k, member * residues : (member + 1) * residues, LANES:] = jnp.broadcast_to(
                    ones, (residues, LANES)
                )

    place = lax.broadcasted_iota(jnp.int32, (1, LANES), 1) // head_size
    blank = jnp.zeros((), BF16)
    members = range(together)
    diagonal = (
        lax.broadcasted_iota(jnp.int32, (residues, owned * width), 0) % owned
        == lax.broadcasted_iota(jnp.int32, (residues, owned * width), 1) // width
    )
    rows = [step * together + k for k in members]
    initial, normed, query, keys, values, gates = [], [], [], [], [], []
    classes_iota = lax.broadcasted_iota(jnp.int32, (padded, residues), 0)
    for k in members:
        tokens = tokens_ref[pl.ds(rows[k], 1), :]
        onehot = (classes_iota == tokens).astype(F32).astype(BF16)
        onehot = jnp.concatenate([onehot, onehot, onehot], axis=0)
        initial.append(dot(onehot, embed_scr[...], ((0,), (0,))) + target_ref[...])
    for k in members:
        normed.append(normalize(initial[k], gain_ref[...]).astype(BF16))
    for k in members:
        product = dot(normed[k], query_ref[...], ((1,), (0,)))
        query.append((product * (1.0 / head_size**0.5)).astype(BF16))
        keys.append(dot(normed[k], key_ref[...], ((1,), (0,))).astype(BF16))
        values.append(dot(normed[k], value_ref[...], ((1,), (0,))).astype(BF16))
    mixed = [[] for _ in members]
    for group in range(groups):
        lanes = slice(group * LANES, (group + 1) * LANES)
        for member in range(packed):
            mine = place == member
            columns = slice(member * residues, (member + 1) * residues)
            for k in members:
                one_query = jnp.where(mine, query[k][:, lanes], blank)
                scores = dot(one_query, keys[k][:, lanes], ((1,), (1,)))
                scores = scores + bias_scr[group * packed + member]
                expo = jnp.exp(scores - jnp.max(scores, axis=-1, keepdims=True))
                weights_scr[k, :, columns] = expo.astype(BF16)
                mixer_scr[k, columns, 0:LANES] = jnp.where(mine, values[k][:, lanes], blank)
        for k in members:
            both = dot(weights_scr[k], mixer_scr[k], ((1,), (0,)))
            mixed[k].append(both[:, :LANES] / both[:, LANES:])
    for k in members:
        gates.append(jax.nn.sigmoid(dot(normed[k], gate_ref[...], ((1,), (0,))) + gate_bias_ref[...]))
    for k in members:
        whole = (jnp.concatenate(mixed[k], axis=1) * gates[k]).astype(BF16)
        updated = initial[k] + dot(whole, output_ref[...], ((1,), (0,)))
        updated_ref[k] = updated
        normed_two = normalize(updated, gain_two_ref[...])
        narrow = normed_two.astype(BF16)
        spread_left = dot(narrow, left_scr[...], ((1,), (1,)))
        spread_left = jnp.where(diagonal, spread_left, 0.0).astype(BF16)
        folded = dot(gather_scr[...], spread_left, ((1,), (0,)))
        for tile in range(owned * width // LANES):
            lanes = slice(tile * LANES, (tile + 1) * LANES)
            owner_scr[tile, pl.ds(rows[k], owners, stride=count), :] = folded[:, lanes]
        right = dot(right_ref[...], narrow, ((1,), (1,)))
        for tile in range(residues // LANES):
            lanes = slice(tile * LANES, (tile + 1) * LANES)
            factor_scr[tile, pl.ds(rows[k], width, stride=count), :] = right[:, lanes]

    @pl.when(step == pl.num_programs(0) - 1)
    def finish():
        right = jnp.concatenate([factor_scr[t] for t in range(residues // LANES)], axis=1)
        right = right.astype(BF16).reshape(width, count, residues)
        mine = lax.axis_index("wide") // inner
        per = residues // LANES
        for shift, message_ref in enumerate(message_refs):
            target = meet(mine, shift, outer) * inner
            message_ref[0:width] = right
            for k in range(inner):
                start = pl.multiple_of((target + k) * count, count)
                for slab in range(slabs):
                    block = [owner_scr[slab * per + t, pl.ds(start, count), :] for t in range(per)]
                    message_ref[width + k * slabs + slab] = jnp.concatenate(block, axis=1).astype(BF16)


def attention(operands, heads, owners, outer):
    tokens, _, target, embed, _, query_weight = operands[:6]
    _, right_weight = operands[13:15]
    count, residues = tokens.shape
    features = target.shape[1]
    head_size = query_weight.shape[1] // heads
    packed = LANES // head_size
    width = right_weight.shape[0]
    owned = residues // owners
    padded = -(-embed.shape[0] // 32) * 32
    together = 2 if count % 2 == 0 else 1
    whole = lambda x: pl.BlockSpec(x.shape, lambda s, n=x.ndim: (0,) * n)
    slabs = owned * width // residues
    message = (width + owners // outer * slabs, count, residues)
    outs = (jax.ShapeDtypeStruct((count, residues, features), F32),) + (
        jax.ShapeDtypeStruct(message, BF16),
    ) * outer
    scratch = [
        ((heads, residues, residues), F32),
        ((heads, LANES), F32),
        ((3 * padded, features), BF16),
        ((owned * width, features), BF16),
        ((together, residues, packed * residues), BF16),
        ((together, packed * residues, 2 * LANES), BF16),
        ((residues // LANES, width * count, LANES), F32),
        ((owned * width // LANES, owners * count, LANES), F32),
        ((owners, residues), BF16),
    ]
    return pl.pallas_call(
        functools.partial(attention_kernel, heads, owners, outer, together),
        grid=(count // together,),
        in_specs=[whole(x) for x in operands],
        out_specs=(pl.BlockSpec((together, residues, features), lambda s: (s, 0, 0)),)
        + tuple(whole(x) for x in outs[1:]),
        out_shape=outs,
        scratch_shapes=[pltpu.VMEM(shape, dtype) for shape, dtype in scratch],
        cost_estimate=pl.CostEstimate(
            flops=count * residues * (8 * features * features + 8 * heads * residues * LANES),
            transcendentals=count * heads * residues * residues,
            bytes_accessed=4 * count * residues * features,
        ),
        name="attention",
    )(*operands)


def spread(messages, devices):
    outer = len(messages)
    inner = devices // outer
    core = 2 if inner % 2 == 0 else 1

    def move(piece, target):
        return lax.ppermute(piece, "wide", [(d, target(d)) for d in range(devices)])

    pieces = [messages[0]] + [
        move(message, lambda d, k=shift: meet(d // inner, k, outer) * inner + d % inner)
        for shift, message in enumerate(messages)
        if shift
    ]
    for axis, stride in ((inner // core, core), (core, 1)):
        pieces = pieces + [
            move(piece, lambda d, k=shift: d + ((d // stride + k) % axis - d // stride % axis) * stride)
            for shift in range(1, axis)
            for piece in pieces
        ]
    return pieces


def order_kernel(weight_ref, own_ref, out_ref, kept_ref, wide_scr, sem):
    width = round(weight_ref.shape[0] ** 0.5)
    copy = pltpu.make_async_copy(own_ref, kept_ref, sem)
    copy.start()
    wide_scr[...] = weight_ref[...].astype(F32)
    for e in range(width):
        out_ref[:, e * width : (e + 1) * width] = wide_scr[pl.ds(e, width, stride=width), :].T.astype(BF16)
    copy.wait()


def ordered(weight, own):
    shape = weight.shape[::-1]
    return pl.pallas_call(
        order_kernel,
        in_specs=[pl.BlockSpec(weight.shape, lambda: (0, 0)), pl.BlockSpec(memory_space=pl.ANY)],
        out_shape=(jax.ShapeDtypeStruct(shape, BF16), jax.ShapeDtypeStruct(own.shape, own.dtype)),
        scratch_shapes=[pltpu.VMEM(weight.shape, F32), pltpu.SemaphoreType.DMA],
        compiler_params=pltpu.CompilerParams(vmem_limit_bytes=8 * 2**20),
        cost_estimate=pl.CostEstimate(flops=0, transcendentals=0, bytes_accessed=4 * math.prod(shape)),
        name="order",
    )(weight, own)


def pair_kernel(count, halves, inner, weight_ref, bias_ref, *rest_refs):
    pieces = len(rest_refs) - 6
    piece_refs = rest_refs[:pieces]
    out_ref, right_scr, left_scr, flat_scr, outer_scr, sems = rest_refs[pieces:]
    groups, depth, residues = right_scr.shape
    height = halves * count
    width = groups * halves
    block = out_ref.shape[0]
    half = flat_scr.shape[1] // halves
    slabs = left_scr.shape[0]

    @pl.when(pl.program_id(0) == 0)
    def prepare():
        mine = lax.rem(lax.axis_index("wide"), inner) * slabs + groups
        copies = []
        for number, piece_ref in enumerate(piece_refs):
            rows = pl.ds(number * height, height)
            copies.append(
                pltpu.make_async_copy(
                    piece_ref.at[pl.ds(mine, slabs)], left_scr.at[:, rows], sems.at[0, number]
                )
            )
            copies.append(
                pltpu.make_async_copy(
                    piece_ref.at[pl.ds(0, groups)], right_scr.at[:, rows], sems.at[1, number]
                )
            )
        for copy in copies:
            copy.start()
        for copy in copies[0::2]:
            copy.wait()
        left = jnp.concatenate([left_scr[slab] for slab in range(slabs)], axis=1)[:, 0:half].astype(F32)
        member = lax.broadcasted_iota(jnp.int32, (depth, 1), 0) % height // count
        for e in range(halves):
            for h in range(halves):
                moved = left
                if e != h:
                    moved = pltpu.roll(left.reshape(pieces, height, half), (e - h) % halves * count, 1)
                    moved = moved.reshape(depth, half)
                moved = jnp.where(member == e, moved, 0.0)
                flat_scr[e, h * half : (h + 1) * half, :] = moved.T.astype(BF16)
        for copy in copies[1::2]:
            copy.wait()

    rows = block * width
    start = pl.multiple_of(pl.program_id(0) * rows, rows)
    for group in range(groups):
        for e in range(halves):
            product = dot(flat_scr[e, pl.ds(start, rows), :], right_scr[group], ((1,), (0,))).astype(BF16)
            place = (group * halves + e) * width
            outer_scr[:, place : place + width, :] = product.reshape(block, width, residues)
    total = float(pieces * count)
    for i in range(block):
        projected = dot(weight_ref[...], outer_scr[i], ((1,), (0,)))
        out_ref[i] = projected.T * (1.0 / total) + bias_ref[...]


def pair_features(pieces, weight, bias, count, inner, owned, blocks):
    slabs, height, residues = pieces[0].shape
    halves = height // count
    width = round(weight.shape[1] ** 0.5)
    groups = width // halves
    slabs = (slabs - groups) // inner
    depth = len(pieces) * height
    channels = weight.shape[0]
    block = owned // blocks
    scratch = [
        ((groups, depth, residues), BF16),
        ((slabs, depth, residues), BF16),
        ((halves, owned * width, depth), BF16),
        ((block, width * width, residues), BF16),
    ]
    used = room(scratch) + 2 * room([(weight.shape, BF16), ((block, residues, channels), F32)])
    return pl.pallas_call(
        functools.partial(pair_kernel, count, halves, inner),
        grid=(blocks,),
        in_specs=[
            pl.BlockSpec(weight.shape, lambda i: (0, 0)),
            pl.BlockSpec((1, channels), lambda i: (0, 0)),
        ]
        + [pl.BlockSpec(memory_space=pl.ANY)] * len(pieces),
        out_specs=pl.BlockSpec((block, residues, channels), lambda i: (i, 0, 0)),
        out_shape=jax.ShapeDtypeStruct((owned, residues, channels), F32),
        scratch_shapes=[pltpu.VMEM(shape, dtype) for shape, dtype in scratch]
        + [pltpu.SemaphoreType.DMA((2, len(pieces)))],
        compiler_params=pltpu.CompilerParams(vmem_limit_bytes=used + 12 * 2**20),
        name="pair",
    )(weight, bias.reshape(1, -1), *pieces)


def shards(
    alignment_token_ids,
    residue_index_offsets,
    target_residue_feature,
    token_embedding_table,
    attention_norm_gain,
    query_weight,
    key_weight,
    value_weight,
    gate_weight,
    gate_offset_bias,
    output_weight,
    relative_position_table,
    product_norm_gain,
    left_weight,
    right_weight,
    pair_weight,
    pair_projection_bias,
):
    devices = lax.axis_size("wide")
    inner = nearest(devices)
    sequences, residues = alignment_token_ids.shape
    operands = (
        alignment_token_ids,
        residue_index_offsets.reshape(1, -1),
        target_residue_feature,
        token_embedding_table,
        attention_norm_gain.reshape(1, -1),
        query_weight,
        key_weight,
        value_weight,
        gate_weight,
        gate_offset_bias.reshape(1, -1),
        output_weight,
        relative_position_table.T,
        product_norm_gain.reshape(1, -1),
        left_weight.T,
        right_weight.T,
    )
    heads = relative_position_table.shape[1]
    updated, *messages = attention(operands, heads, devices, devices // inner)
    pieces = spread(messages, devices)
    weight, pieces[0] = ordered(pair_weight, messages[0])
    pair = pair_features(
        pieces,
        weight,
        pair_projection_bias,
        sequences,
        inner,
        residues // devices,
        2,
    )
    return (updated, pair)


def solution(mesh):
    placed = (P(("groups", "wide"), None), P("groups"), P("groups", None)) + (P(),) * 14
    return jax.shard_map(
        shards,
        mesh=mesh,
        in_specs=placed,
        out_specs=(P(("groups", "wide"), None, None), P(("groups", "wide"), None, None)),
        check_vma=False,
    )
```

```python
import functools
import math

import jax
import jax.numpy as jnp
from jax import lax
from jax.experimental import pallas as pl
from jax.experimental.pallas import tpu as pltpu
from jax.sharding import PartitionSpec as P


REACH = 32
LANES = 128
F32 = jnp.float32
BF16 = jnp.bfloat16


def dot(a, b, axes):
    return lax.dot_general(a, b, (axes, ((), ())), preferred_element_type=F32)


def normalize(values, gain):
    center = jnp.mean(values, axis=-1, keepdims=True)
    centred = values - center
    spread = jnp.mean(centred * centred, axis=-1, keepdims=True)
    return centred * lax.rsqrt(spread + 1e-05) * gain


def meet(place, shift, size):
    if size & (size - 1):
        return (place + shift) % size
    return place ^ shift


def nearest(devices):
    core = 2 if devices % 2 == 0 else 1
    return 2 * core if devices % (2 * core) == 0 else core


def room(shapes):
    total = 0
    for shape, dtype in shapes:
        total += math.prod(shape) * jnp.dtype(dtype).itemsize
    return total


def attention_kernel(heads, owners, outer, together, *refs):
    (
        tokens_ref,
        offsets_ref,
        target_ref,
        embed_ref,
        gain_ref,
        query_ref,
        key_ref,
        value_ref,
        gate_ref,
        gate_bias_ref,
        output_ref,
        relative_ref,
        gain_two_ref,
        left_ref,
        right_ref,
    ) = refs[:15]
    updated_ref, *rest_refs = refs[15:]
    message_refs = rest_refs[:outer]
    (
        bias_scr,
        relative_scr,
        embed_scr,
        left_scr,
        weights_scr,
        mixer_scr,
        factor_scr,
        owner_scr,
        gather_scr,
        narrow_scr,
        sorted_scr,
    ) = rest_refs[outer:]
    step = pl.program_id(0)
    residues, features = target_ref.shape
    head_size = query_ref.shape[1] // heads
    packed = LANES // head_size
    groups = heads // packed
    classes = embed_ref.shape[0]
    padded = embed_scr.shape[0] // 3
    width = right_ref.shape[0]
    bins = relative_ref.shape[1]
    inner = owners // outer
    owned = residues // owners
    count = factor_scr.shape[1] // width
    slabs = owned * width // residues

    @pl.when(step == 0)
    def prepare():
        relative_scr[...] = jnp.zeros_like(relative_scr)
        relative_scr[0:heads, 0:bins] = relative_ref[...]
        table = relative_scr[...]
        row = offsets_ref[...]
        column = jnp.broadcast_to(row, (LANES, residues)).T
        for block in range(residues // LANES):
            lanes = slice(block * LANES, (block + 1) * LANES)
            start, stop = block * LANES, (block + 1) * LANES
            low = max(0, (start - REACH + 1) // 8 * 8)
            high = min(residues, -(-(stop + REACH) // 8) * 8)
            for tile in range(low, high, 8):
                rows = slice(tile, tile + 8)
                index = jnp.clip(row[:, lanes] - column[rows], -REACH, REACH) + REACH
                for head in range(heads):
                    source = jnp.broadcast_to(table[head : head + 1, :], (8, LANES))
                    bias_scr[head, rows, lanes] = jnp.take_along_axis(source, index, axis=1)
            for head in range(heads):
                if low:
                    after = table[head : head + 1, 2 * REACH : 2 * REACH + 1]
                    bias_scr[head, 0:low, lanes] = jnp.broadcast_to(after, (low, LANES))
                if high < residues:
                    before = table[head : head + 1, 0:1]
                    bias_scr[head, high:, lanes] = jnp.broadcast_to(before, (residues - high, LANES))
        embed_scr[...] = jnp.zeros_like(embed_scr)
        embed = embed_ref[...]
        high = embed.astype(BF16)
        rest = embed - high.astype(F32)
        middle = rest.astype(BF16)
        low = (rest - middle.astype(F32)).astype(BF16)
        for part, piece in enumerate((high, middle, low)):
            embed_scr[part * padded : part * padded + classes, :] = piece
        left_scr[...] = jnp.zeros_like(left_scr)
        for tile in range(LANES // width):
            left_scr[tile, tile * width : (tile + 1) * width, :] = left_ref[...]
        target_row = lax.broadcasted_iota(jnp.int32, gather_scr.shape, 0)
        gather_scr[...] = (
            target_row % owners * owned + target_row // owners
            == lax.broadcasted_iota(jnp.int32, gather_scr.shape, 1)
        ).astype(F32).astype(BF16)
        place = lax.broadcasted_iota(jnp.int32, (1, LANES), 1) // head_size
        for member in range(packed):
            ones = jnp.where(place == member, jnp.ones((), BF16), jnp.zeros((), BF16))
            for k in range(together):
                mixer_scr[k, member * residues : (member + 1) * residues, LANES:] = jnp.broadcast_to(
                    ones, (residues, LANES)
                )

    place = lax.broadcasted_iota(jnp.int32, (1, LANES), 1) // head_size
    blank = jnp.zeros((), BF16)
    members = range(together)
    rows = [step * together + k for k in members]
    initial, normed, query, keys, values, gates = [], [], [], [], [], []
    classes_iota = lax.broadcasted_iota(jnp.int32, (padded, residues), 0)
    for k in members:
        tokens = tokens_ref[pl.ds(rows[k], 1), :]
        onehot = (classes_iota == tokens).astype(F32).astype(BF16)
        onehot = jnp.concatenate([onehot, onehot, onehot], axis=0)
        initial.append(dot(onehot, embed_scr[...], ((0,), (0,))) + target_ref[...])
    for k in members:
        normed.append(normalize(initial[k], gain_ref[...]).astype(BF16))
    for k in members:
        product = dot(normed[k], query_ref[...], ((1,), (0,)))
        query.append((product * (1.0 / head_size**0.5)).astype(BF16))
        keys.append(dot(normed[k], key_ref[...], ((1,), (0,))).astype(BF16))
        values.append(dot(normed[k], value_ref[...], ((1,), (0,))).astype(BF16))
    mixed = [[] for _ in members]
    for group in range(groups):
        lanes = slice(group * LANES, (group + 1) * LANES)
        for member in range(packed):
            mine = place == member
            columns = slice(member * residues, (member + 1) * residues)
            for k in members:
                one_query = jnp.where(mine, query[k][:, lanes], blank)
                scores = dot(one_query, keys[k][:, lanes], ((1,), (1,)))
                scores = scores + bias_scr[group * packed + member]
                expo = jnp.exp(scores - jnp.max(scores, axis=-1, keepdims=True))
                weights_scr[k, :, columns] = expo.astype(BF16)
                mixer_scr[k, columns, 0:LANES] = jnp.where(mine, values[k][:, lanes], blank)
        for k in members:
            both = dot(weights_scr[k], mixer_scr[k], ((1,), (0,)))
            mixed[k].append(both[:, :LANES] / both[:, LANES:])
    for k in members:
        gates.append(jax.nn.sigmoid(dot(normed[k], gate_ref[...], ((1,), (0,))) + gate_bias_ref[...]))
    for k in members:
        whole = (jnp.concatenate(mixed[k], axis=1) * gates[k]).astype(BF16)
        updated = initial[k] + dot(whole, output_ref[...], ((1,), (0,)))
        updated_ref[k] = updated
        normed_two = normalize(updated, gain_two_ref[...])
        narrow_scr[rows[k]] = normed_two.astype(BF16)

    @pl.when(step == pl.num_programs(0) - 1)
    def finish():
        for k in range(count):
            narrow = narrow_scr[k]
            sorted_rows = dot(gather_scr[...], narrow, ((1,), (0,))).astype(BF16)
            sorted_scr[:, k] = sorted_rows.reshape(owned, owners, features)
            right = dot(right_ref[...], narrow, ((1,), (1,)))
            for tile in range(residues // LANES):
                lanes = slice(tile * LANES, (tile + 1) * LANES)
                factor_scr[tile, pl.ds(k, width, stride=count), :] = right[:, lanes]
        fold = LANES // width
        for tile in range(owned // fold):
            total = jnp.zeros((count * owners, LANES), F32)
            for place in range(fold):
                one = sorted_scr[tile * fold + place].reshape(count * owners, features)
                total += dot(one, left_scr[place], ((1,), (1,)))
            owner_scr[tile] = total
        right = jnp.concatenate([factor_scr[t] for t in range(residues // LANES)], axis=1)
        right = right.astype(BF16).reshape(width, count, residues)
        mine = lax.axis_index("wide") // inner
        per = residues // LANES
        for shift, message_ref in enumerate(message_refs):
            target = meet(mine, shift, outer) * inner
            message_ref[0:width] = right
            for k in range(inner):
                for slab in range(slabs):
                    block = [
                        owner_scr[slab * per + t, pl.ds(target + k, count, stride=owners), :] for t in range(per)
                    ]
                    message_ref[width + k * slabs + slab] = jnp.concatenate(block, axis=1).astype(BF16)


def attention(operands, heads, owners, outer):
    tokens, _, target, embed, _, query_weight = operands[:6]
    _, right_weight = operands[13:15]
    count, residues = tokens.shape
    features = target.shape[1]
    head_size = query_weight.shape[1] // heads
    packed = LANES // head_size
    width = right_weight.shape[0]
    owned = residues // owners
    padded = -(-embed.shape[0] // 32) * 32
    together = 2 if count % 2 == 0 else 1
    whole = lambda x: pl.BlockSpec(x.shape, lambda s, n=x.ndim: (0,) * n)
    slabs = owned * width // residues
    message = (width + owners // outer * slabs, count, residues)
    outs = (jax.ShapeDtypeStruct((count, residues, features), F32),) + (
        jax.ShapeDtypeStruct(message, BF16),
    ) * outer
    scratch = [
        ((heads, residues, residues), F32),
        ((heads, LANES), F32),
        ((3 * padded, features), BF16),
        ((LANES // width, LANES, features), BF16),
        ((together, residues, packed * residues), BF16),
        ((together, packed * residues, 2 * LANES), BF16),
        ((residues // LANES, width * count, LANES), F32),
        ((owned * width // LANES, owners * count, LANES), F32),
        ((residues, residues), BF16),
        ((count, residues, features), BF16),
        ((owned, count, owners, features), BF16),
    ]
    return pl.pallas_call(
        functools.partial(attention_kernel, heads, owners, outer, together),
        grid=(count // together,),
        in_specs=[whole(x) for x in operands],
        out_specs=(pl.BlockSpec((together, residues, features), lambda s: (s, 0, 0)),)
        + tuple(whole(x) for x in outs[1:]),
        out_shape=outs,
        scratch_shapes=[pltpu.VMEM(shape, dtype) for shape, dtype in scratch],
        cost_estimate=pl.CostEstimate(
            flops=count * residues * (8 * features * features + 8 * heads * residues * LANES),
            transcendentals=count * heads * residues * residues,
            bytes_accessed=4 * count * residues * features,
        ),
        name="attention",
    )(*operands)


def spread(messages, devices):
    outer = len(messages)
    inner = devices // outer
    core = 2 if inner % 2 == 0 else 1

    def move(piece, target):
        return lax.ppermute(piece, "wide", [(d, target(d)) for d in range(devices)])

    pieces = [messages[0]] + [
        move(message, lambda d, k=shift: meet(d // inner, k, outer) * inner + d % inner)
        for shift, message in enumerate(messages)
        if shift
    ]
    for axis, stride in ((inner // core, core), (core, 1)):
        pieces = pieces + [
            move(piece, lambda d, k=shift: d + ((d // stride + k) % axis - d // stride % axis) * stride)
            for shift in range(1, axis)
            for piece in pieces
        ]
    return pieces


def order_kernel(weight_ref, own_ref, out_ref, kept_ref, wide_scr, sem):
    width = round(weight_ref.shape[0] ** 0.5)
    copy = pltpu.make_async_copy(own_ref, kept_ref, sem)
    copy.start()
    wide_scr[...] = weight_ref[...].astype(F32)
    for e in range(width):
        out_ref[:, e * width : (e + 1) * width] = wide_scr[pl.ds(e, width, stride=width), :].T.astype(BF16)
    copy.wait()


def ordered(weight, own):
    shape = weight.shape[::-1]
    return pl.pallas_call(
        order_kernel,
        in_specs=[pl.BlockSpec(weight.shape, lambda: (0, 0)), pl.BlockSpec(memory_space=pl.ANY)],
        out_shape=(jax.ShapeDtypeStruct(shape, BF16), jax.ShapeDtypeStruct(own.shape, own.dtype)),
        scratch_shapes=[pltpu.VMEM(weight.shape, F32), pltpu.SemaphoreType.DMA],
        compiler_params=pltpu.CompilerParams(vmem_limit_bytes=8 * 2**20),
        cost_estimate=pl.CostEstimate(flops=0, transcendentals=0, bytes_accessed=4 * math.prod(shape)),
        name="order",
    )(weight, own)


def pair_kernel(count, halves, inner, weight_ref, bias_ref, *rest_refs):
    pieces = len(rest_refs) - 6
    piece_refs = rest_refs[:pieces]
    out_ref, right_scr, left_scr, flat_scr, outer_scr, sems = rest_refs[pieces:]
    groups, depth, residues = right_scr.shape
    height = halves * count
    width = groups * halves
    block = out_ref.shape[0]
    half = flat_scr.shape[1] // halves
    slabs = left_scr.shape[0]

    @pl.when(pl.program_id(0) == 0)
    def prepare():
        mine = lax.rem(lax.axis_index("wide"), inner) * slabs + groups
        copies = []
        for number, piece_ref in enumerate(piece_refs):
            rows = pl.ds(number * height, height)
            copies.append(
                pltpu.make_async_copy(
                    piece_ref.at[pl.ds(mine, slabs)], left_scr.at[:, rows], sems.at[0, number]
                )
            )
            copies.append(
                pltpu.make_async_copy(
                    piece_ref.at[pl.ds(0, groups)], right_scr.at[:, rows], sems.at[1, number]
                )
            )
        for copy in copies:
            copy.start()
        for copy in copies[0::2]:
            copy.wait()
        left = jnp.concatenate([left_scr[slab] for slab in range(slabs)], axis=1)[:, 0:half].astype(F32)
        member = lax.broadcasted_iota(jnp.int32, (depth, 1), 0) % height // count
        for e in range(halves):
            for h in range(halves):
                moved = left
                if e != h:
                    moved = pltpu.roll(left.reshape(pieces, height, half), (e - h) % halves * count, 1)
                    moved = moved.reshape(depth, half)
                moved = jnp.where(member == e, moved, 0.0)
                flat_scr[e, h * half : (h + 1) * half, :] = moved.T.astype(BF16)
        for copy in copies[1::2]:
            copy.wait()

    rows = block * width
    start = pl.multiple_of(pl.program_id(0) * rows, rows)
    for group in range(groups):
        for e in range(halves):
            product = dot(flat_scr[e, pl.ds(start, rows), :], right_scr[group], ((1,), (0,))).astype(BF16)
            place = (group * halves + e) * width
            outer_scr[:, place : place + width, :] = product.reshape(block, width, residues)
    total = float(pieces * count)
    for i in range(block):
        projected = dot(weight_ref[...], outer_scr[i], ((1,), (0,)))
        out_ref[i] = projected.T * (1.0 / total) + bias_ref[...]


def pair_features(pieces, weight, bias, count, inner, owned, blocks):
    slabs, height, residues = pieces[0].shape
    halves = height // count
    width = round(weight.shape[1] ** 0.5)
    groups = width // halves
    slabs = (slabs - groups) // inner
    depth = len(pieces) * height
    channels = weight.shape[0]
    block = owned // blocks
    scratch = [
        ((groups, depth, residues), BF16),
        ((slabs, depth, residues), BF16),
        ((halves, owned * width, depth), BF16),
        ((block, width * width, residues), BF16),
    ]
    used = room(scratch) + 2 * room([(weight.shape, BF16), ((block, residues, channels), F32)])
    return pl.pallas_call(
        functools.partial(pair_kernel, count, halves, inner),
        grid=(blocks,),
        in_specs=[
            pl.BlockSpec(weight.shape, lambda i: (0, 0)),
            pl.BlockSpec((1, channels), lambda i: (0, 0)),
        ]
        + [pl.BlockSpec(memory_space=pl.ANY)] * len(pieces),
        out_specs=pl.BlockSpec((block, residues, channels), lambda i: (i, 0, 0)),
        out_shape=jax.ShapeDtypeStruct((owned, residues, channels), F32),
        scratch_shapes=[pltpu.VMEM(shape, dtype) for shape, dtype in scratch]
        + [pltpu.SemaphoreType.DMA((2, len(pieces)))],
        compiler_params=pltpu.CompilerParams(vmem_limit_bytes=used + 12 * 2**20),
        name="pair",
    )(weight, bias.reshape(1, -1), *pieces)


def shards(
    alignment_token_ids,
    residue_index_offsets,
    target_residue_feature,
    token_embedding_table,
    attention_norm_gain,
    query_weight,
    key_weight,
    value_weight,
    gate_weight,
    gate_offset_bias,
    output_weight,
    relative_position_table,
    product_norm_gain,
    left_weight,
    right_weight,
    pair_weight,
    pair_projection_bias,
):
    devices = lax.axis_size("wide")
    inner = nearest(devices)
    sequences, residues = alignment_token_ids.shape
    operands = (
        alignment_token_ids,
        residue_index_offsets.reshape(1, -1),
        target_residue_feature,
        token_embedding_table,
        attention_norm_gain.reshape(1, -1),
        query_weight,
        key_weight,
        value_weight,
        gate_weight,
        gate_offset_bias.reshape(1, -1),
        output_weight,
        relative_position_table.T,
        product_norm_gain.reshape(1, -1),
        left_weight.T,
        right_weight.T,
    )
    heads = relative_position_table.shape[1]
    updated, *messages = attention(operands, heads, devices, devices // inner)
    pieces = spread(messages, devices)
    weight, pieces[0] = ordered(pair_weight, messages[0])
    pair = pair_features(
        pieces,
        weight,
        pair_projection_bias,
        sequences,
        inner,
        residues // devices,
        2,
    )
    return (updated, pair)


def solution(mesh):
    placed = (P(("groups", "wide"), None), P("groups"), P("groups", None)) + (P(),) * 14
    return jax.shard_map(
        shards,
        mesh=mesh,
        in_specs=placed,
        out_specs=(P(("groups", "wide"), None, None), P(("groups", "wide"), None, None)),
        check_vma=False,
    )
```

```python
import functools
import math

import jax
import jax.numpy as jnp
from jax import lax
from jax.experimental import pallas as pl
from jax.experimental.pallas import tpu as pltpu
from jax.sharding import PartitionSpec as P


REACH = 32
LANES = 128
ROWS = 1024
F32 = jnp.float32
BF16 = jnp.bfloat16


def dot(a, b, axes):
    return lax.dot_general(a, b, (axes, ((), ())), preferred_element_type=F32)


def normalize(values, gain):
    center = jnp.mean(values, axis=-1, keepdims=True)
    centred = values - center
    spread = jnp.mean(centred * centred, axis=-1, keepdims=True)
    return centred * lax.rsqrt(spread + 1e-05) * gain


def meet(place, shift, size):
    if size & (size - 1):
        return (place + shift) % size
    return place ^ shift


def nearest(devices):
    core = 2 if devices % 2 == 0 else 1
    return 2 * core if devices % (2 * core) == 0 else core


def room(shapes):
    total = 0
    for shape, dtype in shapes:
        total += math.prod(shape) * jnp.dtype(dtype).itemsize
    return total


def attention_kernel(heads, owners, outer, together, *refs):
    (
        tokens_ref,
        offsets_ref,
        target_ref,
        embed_ref,
        gain_ref,
        query_ref,
        key_ref,
        value_ref,
        gate_ref,
        gate_bias_ref,
        output_ref,
        relative_ref,
        gain_two_ref,
        left_ref,
        right_ref,
    ) = refs[:15]
    updated_ref, *rest_refs = refs[15:]
    message_refs = rest_refs[:outer]
    (
        bias_scr,
        relative_scr,
        embed_scr,
        left_scr,
        weights_scr,
        mixer_scr,
        factor_scr,
        owner_scr,
        gather_scr,
        narrow_scr,
        sorted_scr,
    ) = rest_refs[outer:]
    step = pl.program_id(0)
    residues, features = target_ref.shape
    head_size = query_ref.shape[1] // heads
    packed = LANES // head_size
    groups = heads // packed
    classes = embed_ref.shape[0]
    padded = embed_scr.shape[0] // 3
    width = right_ref.shape[0]
    bins = relative_ref.shape[1]
    inner = owners // outer
    owned = residues // owners
    count = factor_scr.shape[1] // width
    slabs = owned * width // residues

    @pl.when(step == 0)
    def prepare():
        relative_scr[...] = jnp.zeros_like(relative_scr)
        relative_scr[0:heads, 0:bins] = relative_ref[...]
        table = relative_scr[...]
        row = offsets_ref[...]
        column = jnp.broadcast_to(row, (LANES, residues)).T
        for block in range(residues // LANES):
            lanes = slice(block * LANES, (block + 1) * LANES)
            start, stop = block * LANES, (block + 1) * LANES
            low = max(0, (start - REACH + 1) // 8 * 8)
            high = min(residues, -(-(stop + REACH) // 8) * 8)
            for tile in range(low, high, 8):
                rows = slice(tile, tile + 8)
                index = jnp.clip(row[:, lanes] - column[rows], -REACH, REACH) + REACH
                for head in range(heads):
                    source = jnp.broadcast_to(table[head : head + 1, :], (8, LANES))
                    bias_scr[head, rows, lanes] = jnp.take_along_axis(source, index, axis=1)
            for head in range(heads):
                if low:
                    after = table[head : head + 1, 2 * REACH : 2 * REACH + 1]
                    bias_scr[head, 0:low, lanes] = jnp.broadcast_to(after, (low, LANES))
                if high < residues:
                    before = table[head : head + 1, 0:1]
                    bias_scr[head, high:, lanes] = jnp.broadcast_to(before, (residues - high, LANES))
        embed_scr[...] = jnp.zeros_like(embed_scr)
        embed = embed_ref[...]
        high = embed.astype(BF16)
        rest = embed - high.astype(F32)
        middle = rest.astype(BF16)
        low = (rest - middle.astype(F32)).astype(BF16)
        for part, piece in enumerate((high, middle, low)):
            embed_scr[part * padded : part * padded + classes, :] = piece
        left_scr[...] = jnp.zeros_like(left_scr)
        for tile in range(LANES // width):
            left_scr[tile, tile * width : (tile + 1) * width, :] = left_ref[...]
        target_row = lax.broadcasted_iota(jnp.int32, gather_scr.shape, 0)
        gather_scr[...] = (
            target_row % owners * owned + target_row // owners
            == lax.broadcasted_iota(jnp.int32, gather_scr.shape, 1)
        ).astype(F32).astype(BF16)
        place = lax.broadcasted_iota(jnp.int32, (1, LANES), 1) // head_size
        for member in range(packed):
            ones = jnp.where(place == member, jnp.ones((), BF16), jnp.zeros((), BF16))
            for k in range(together):
                mixer_scr[k, member * residues : (member + 1) * residues, LANES:] = jnp.broadcast_to(
                    ones, (residues, LANES)
                )

    place = lax.broadcasted_iota(jnp.int32, (1, LANES), 1) // head_size
    blank = jnp.zeros((), BF16)
    members = range(together)
    rows = [step * together + k for k in members]
    initial, query, keys, values, gates = [], [], [], [], []
    classes_iota = lax.broadcasted_iota(jnp.int32, (padded, residues), 0)
    for k in members:
        tokens = tokens_ref[pl.ds(rows[k], 1), :]
        onehot = (classes_iota == tokens).astype(F32).astype(BF16)
        onehot = jnp.concatenate([onehot, onehot, onehot], axis=0)
        initial.append(dot(onehot, embed_scr[...], ((0,), (0,))) + target_ref[...])
    both_initial = jnp.concatenate(initial, axis=0)
    both_normed = normalize(both_initial, gain_ref[...]).astype(BF16)
    spans = [slice(k * residues, (k + 1) * residues) for k in members]
    product = dot(both_normed, query_ref[...], ((1,), (0,)))
    product = (product * (1.0 / head_size**0.5)).astype(BF16)
    query = [product[span] for span in spans]
    product = dot(both_normed, key_ref[...], ((1,), (0,))).astype(BF16)
    keys = [product[span] for span in spans]
    product = dot(both_normed, value_ref[...], ((1,), (0,))).astype(BF16)
    values = [product[span] for span in spans]
    mixed = [[] for _ in members]
    for group in range(groups):
        lanes = slice(group * LANES, (group + 1) * LANES)
        for member in range(packed):
            mine = place == member
            columns = slice(member * residues, (member + 1) * residues)
            for k in members:
                one_query = jnp.where(mine, query[k][:, lanes], blank)
                scores = dot(one_query, keys[k][:, lanes], ((1,), (1,)))
                scores = scores + bias_scr[group * packed + member]
                expo = jnp.exp(scores - jnp.max(scores, axis=-1, keepdims=True))
                weights_scr[k, :, columns] = expo.astype(BF16)
                mixer_scr[k, columns, 0:LANES] = jnp.where(mine, values[k][:, lanes], blank)
        for k in members:
            both = dot(weights_scr[k], mixer_scr[k], ((1,), (0,)))
            mixed[k].append(both[:, :LANES] / both[:, LANES:])
    gates = jax.nn.sigmoid(dot(both_normed, gate_ref[...], ((1,), (0,))) + gate_bias_ref[...])
    whole = jnp.concatenate([jnp.concatenate(mixed[k], axis=1) for k in members], axis=0)
    whole = (whole * gates).astype(BF16)
    updated = both_initial + dot(whole, output_ref[...], ((1,), (0,)))
    normed_two = normalize(updated, gain_two_ref[...]).astype(BF16)
    for k in members:
        updated_ref[k] = updated[spans[k]]
        narrow_scr[rows[k]] = normed_two[spans[k]]

    @pl.when(step == pl.num_programs(0) - 1)
    def finish():
        for k in range(count):
            narrow = narrow_scr[k]
            sorted_rows = dot(gather_scr[...], narrow, ((1,), (0,))).astype(BF16)
            sorted_scr[:, k] = sorted_rows.reshape(owned, owners, features)
            right = dot(right_ref[...], narrow, ((1,), (1,)))
            for tile in range(residues // LANES):
                lanes = slice(tile * LANES, (tile + 1) * LANES)
                factor_scr[tile, pl.ds(k, width, stride=count), :] = right[:, lanes]
        fold = LANES // width
        for tile in range(owned // fold):
            total = jnp.zeros((count * owners, LANES), F32)
            for place in range(fold):
                one = sorted_scr[tile * fold + place].reshape(count * owners, features)
                total += dot(one, left_scr[place], ((1,), (1,)))
            owner_scr[tile] = total
        right = jnp.concatenate([factor_scr[t] for t in range(residues // LANES)], axis=1)
        right = right.astype(BF16).reshape(width, count, residues)
        mine = lax.axis_index("wide") // inner
        per = residues // LANES
        for shift, message_ref in enumerate(message_refs):
            target = meet(mine, shift, outer) * inner
            message_ref[0:width] = right
            for k in range(inner):
                for slab in range(slabs):
                    block = [
                        owner_scr[slab * per + t, pl.ds(target + k, count, stride=owners), :] for t in range(per)
                    ]
                    message_ref[width + k * slabs + slab] = jnp.concatenate(block, axis=1).astype(BF16)


def attention(operands, heads, owners, outer):
    tokens, _, target, embed, _, query_weight = operands[:6]
    _, right_weight = operands[13:15]
    count, residues = tokens.shape
    features = target.shape[1]
    head_size = query_weight.shape[1] // heads
    packed = LANES // head_size
    width = right_weight.shape[0]
    owned = residues // owners
    padded = -(-embed.shape[0] // 32) * 32
    together = math.gcd(count, max(1, ROWS // residues))
    whole = lambda x: pl.BlockSpec(x.shape, lambda s, n=x.ndim: (0,) * n)
    slabs = owned * width // residues
    message = (width + owners // outer * slabs, count, residues)
    outs = (jax.ShapeDtypeStruct((count, residues, features), F32),) + (
        jax.ShapeDtypeStruct(message, BF16),
    ) * outer
    scratch = [
        ((heads, residues, residues), F32),
        ((heads, LANES), F32),
        ((3 * padded, features), BF16),
        ((LANES // width, LANES, features), BF16),
        ((together, residues, packed * residues), BF16),
        ((together, packed * residues, 2 * LANES), BF16),
        ((residues // LANES, width * count, LANES), F32),
        ((owned * width // LANES, owners * count, LANES), F32),
        ((residues, residues), BF16),
        ((count, residues, features), BF16),
        ((owned, count, owners, features), BF16),
    ]
    return pl.pallas_call(
        functools.partial(attention_kernel, heads, owners, outer, together),
        grid=(count // together,),
        in_specs=[whole(x) for x in operands],
        out_specs=(pl.BlockSpec((together, residues, features), lambda s: (s, 0, 0)),)
        + tuple(whole(x) for x in outs[1:]),
        out_shape=outs,
        scratch_shapes=[pltpu.VMEM(shape, dtype) for shape, dtype in scratch],
        cost_estimate=pl.CostEstimate(
            flops=count * residues * (8 * features * features + 8 * heads * residues * LANES),
            transcendentals=count * heads * residues * residues,
            bytes_accessed=4 * count * residues * features,
        ),
        name="attention",
    )(*operands)


def spread(messages, devices):
    outer = len(messages)
    inner = devices // outer
    core = 2 if inner % 2 == 0 else 1

    def move(piece, target):
        return lax.ppermute(piece, "wide", [(d, target(d)) for d in range(devices)])

    pieces = [messages[0]] + [
        move(message, lambda d, k=shift: meet(d // inner, k, outer) * inner + d % inner)
        for shift, message in enumerate(messages)
        if shift
    ]
    for axis, stride in ((inner // core, core), (core, 1)):
        pieces = pieces + [
            move(piece, lambda d, k=shift: d + ((d // stride + k) % axis - d // stride % axis) * stride)
            for shift in range(1, axis)
            for piece in pieces
        ]
    return pieces


def order_kernel(weight_ref, own_ref, out_ref, kept_ref, wide_scr, sem):
    width = round(weight_ref.shape[0] ** 0.5)
    copy = pltpu.make_async_copy(own_ref, kept_ref, sem)
    copy.start()
    wide_scr[...] = weight_ref[...].astype(F32)
    for e in range(width):
        out_ref[:, e * width : (e + 1) * width] = wide_scr[pl.ds(e, width, stride=width), :].T.astype(BF16)
    copy.wait()


def ordered(weight, own):
    shape = weight.shape[::-1]
    return pl.pallas_call(
        order_kernel,
        in_specs=[pl.BlockSpec(weight.shape, lambda: (0, 0)), pl.BlockSpec(memory_space=pl.ANY)],
        out_shape=(jax.ShapeDtypeStruct(shape, BF16), jax.ShapeDtypeStruct(own.shape, own.dtype)),
        scratch_shapes=[pltpu.VMEM(weight.shape, F32), pltpu.SemaphoreType.DMA],
        compiler_params=pltpu.CompilerParams(vmem_limit_bytes=8 * 2**20),
        cost_estimate=pl.CostEstimate(flops=0, transcendentals=0, bytes_accessed=4 * math.prod(shape)),
        name="order",
    )(weight, own)


def pair_kernel(count, halves, inner, weight_ref, bias_ref, *rest_refs):
    pieces = len(rest_refs) - 6
    piece_refs = rest_refs[:pieces]
    out_ref, right_scr, left_scr, flat_scr, outer_scr, sems = rest_refs[pieces:]
    groups, depth, residues = right_scr.shape
    height = halves * count
    width = groups * halves
    block = out_ref.shape[0]
    half = flat_scr.shape[1] // halves
    slabs = left_scr.shape[0]

    @pl.when(pl.program_id(0) == 0)
    def prepare():
        mine = lax.rem(lax.axis_index("wide"), inner) * slabs + groups
        copies = []
        for number, piece_ref in enumerate(piece_refs):
            rows = pl.ds(number * height, height)
            copies.append(
                pltpu.make_async_copy(
                    piece_ref.at[pl.ds(mine, slabs)], left_scr.at[:, rows], sems.at[0, number]
                )
            )
            copies.append(
                pltpu.make_async_copy(
                    piece_ref.at[pl.ds(0, groups)], right_scr.at[:, rows], sems.at[1, number]
                )
            )
        for copy in copies:
            copy.start()
        for copy in copies[0::2]:
            copy.wait()
        left = jnp.concatenate([left_scr[slab] for slab in range(slabs)], axis=1)[:, 0:half].astype(F32)
        member = lax.broadcasted_iota(jnp.int32, (depth, 1), 0) % height // count
        for e in range(halves):
            for h in range(halves):
                moved = left
                if e != h:
                    moved = pltpu.roll(left.reshape(pieces, height, half), (e - h) % halves * count, 1)
                    moved = moved.reshape(depth, half)
                moved = jnp.where(member == e, moved, 0.0)
                flat_scr[e, h * half : (h + 1) * half, :] = moved.T.astype(BF16)
        for copy in copies[1::2]:
            copy.wait()

    rows = block * width
    start = pl.multiple_of(pl.program_id(0) * rows, rows)
    for group in range(groups):
        for e in range(halves):
            product = dot(flat_scr[e, pl.ds(start, rows), :], right_scr[group], ((1,), (0,))).astype(BF16)
            place = (group * halves + e) * width
            outer_scr[:, place : place + width, :] = product.reshape(block, width, residues)
    total = float(pieces * count)
    for i in range(block):
        projected = dot(weight_ref[...], outer_scr[i], ((1,), (0,)))
        out_ref[i] = projected.T * (1.0 / total) + bias_ref[...]


def pair_features(pieces, weight, bias, count, inner, owned, blocks):
    slabs, height, residues = pieces[0].shape
    halves = height // count
    width = round(weight.shape[1] ** 0.5)
    groups = width // halves
    slabs = (slabs - groups) // inner
    depth = len(pieces) * height
    channels = weight.shape[0]
    block = owned // blocks
    scratch = [
        ((groups, depth, residues), BF16),
        ((slabs, depth, residues), BF16),
        ((halves, owned * width, depth), BF16),
        ((block, width * width, residues), BF16),
    ]
    used = room(scratch) + 2 * room([(weight.shape, BF16), ((block, residues, channels), F32)])
    return pl.pallas_call(
        functools.partial(pair_kernel, count, halves, inner),
        grid=(blocks,),
        in_specs=[
            pl.BlockSpec(weight.shape, lambda i: (0, 0)),
            pl.BlockSpec((1, channels), lambda i: (0, 0)),
        ]
        + [pl.BlockSpec(memory_space=pl.ANY)] * len(pieces),
        out_specs=pl.BlockSpec((block, residues, channels), lambda i: (i, 0, 0)),
        out_shape=jax.ShapeDtypeStruct((owned, residues, channels), F32),
        scratch_shapes=[pltpu.VMEM(shape, dtype) for shape, dtype in scratch]
        + [pltpu.SemaphoreType.DMA((2, len(pieces)))],
        compiler_params=pltpu.CompilerParams(vmem_limit_bytes=used + 12 * 2**20),
        name="pair",
    )(weight, bias.reshape(1, -1), *pieces)


def shards(
    alignment_token_ids,
    residue_index_offsets,
    target_residue_feature,
    token_embedding_table,
    attention_norm_gain,
    query_weight,
    key_weight,
    value_weight,
    gate_weight,
    gate_offset_bias,
    output_weight,
    relative_position_table,
    product_norm_gain,
    left_weight,
    right_weight,
    pair_weight,
    pair_projection_bias,
):
    devices = lax.axis_size("wide")
    inner = nearest(devices)
    sequences, residues = alignment_token_ids.shape
    operands = (
        alignment_token_ids,
        residue_index_offsets.reshape(1, -1),
        target_residue_feature,
        token_embedding_table,
        attention_norm_gain.reshape(1, -1),
        query_weight,
        key_weight,
        value_weight,
        gate_weight,
        gate_offset_bias.reshape(1, -1),
        output_weight,
        relative_position_table.T,
        product_norm_gain.reshape(1, -1),
        left_weight.T,
        right_weight.T,
    )
    heads = relative_position_table.shape[1]
    updated, *messages = attention(operands, heads, devices, devices // inner)
    pieces = spread(messages, devices)
    weight, pieces[0] = ordered(pair_weight, messages[0])
    pair = pair_features(
        pieces,
        weight,
        pair_projection_bias,
        sequences,
        inner,
        residues // devices,
        2,
    )
    return (updated, pair)


def solution(mesh):
    placed = (P(("groups", "wide"), None), P("groups"), P("groups", None)) + (P(),) * 14
    return jax.shard_map(
        shards,
        mesh=mesh,
        in_specs=placed,
        out_specs=(P(("groups", "wide"), None, None), P(("groups", "wide"), None, None)),
        check_vma=False,
    )
```

```python
import functools
import math

import jax
import jax.numpy as jnp
from jax import lax
from jax.experimental import pallas as pl
from jax.experimental.pallas import tpu as pltpu
from jax.sharding import PartitionSpec as P


REACH = 32
LANES = 128
ROWS = 1024
F32 = jnp.float32
BF16 = jnp.bfloat16


def dot(a, b, axes):
    return lax.dot_general(a, b, (axes, ((), ())), preferred_element_type=F32)


def normalize(values, gain):
    center = jnp.mean(values, axis=-1, keepdims=True)
    centred = values - center
    spread = jnp.mean(centred * centred, axis=-1, keepdims=True)
    return centred * lax.rsqrt(spread + 1e-05) * gain


def meet(place, shift, size):
    if size & (size - 1):
        return (place + shift) % size
    return place ^ shift


def nearest(devices):
    core = 2 if devices % 2 == 0 else 1
    return 2 * core if devices % (2 * core) == 0 else core


def room(shapes):
    total = 0
    for shape, dtype in shapes:
        total += math.prod(shape) * jnp.dtype(dtype).itemsize
    return total


def attention_kernel(heads, owners, outer, together, *refs):
    (
        tokens_ref,
        offsets_ref,
        target_ref,
        embed_ref,
        gain_ref,
        query_ref,
        key_ref,
        value_ref,
        gate_ref,
        gate_bias_ref,
        output_ref,
        relative_ref,
        gain_two_ref,
        left_ref,
        right_ref,
    ) = refs[:15]
    updated_ref, *rest_refs = refs[15:]
    message_refs = rest_refs[:outer]
    (
        bias_scr,
        relative_scr,
        embed_scr,
        left_scr,
        weights_scr,
        mixer_scr,
        factor_scr,
        owner_scr,
        gather_scr,
        narrow_scr,
        sorted_scr,
    ) = rest_refs[outer:]
    step = pl.program_id(0)
    residues, features = target_ref.shape
    head_size = query_ref.shape[1] // heads
    packed = LANES // head_size
    groups = heads // packed
    classes = embed_ref.shape[0]
    padded = embed_scr.shape[0] // 3
    width = right_ref.shape[0]
    bins = relative_ref.shape[1]
    inner = owners // outer
    owned = residues // owners
    count = factor_scr.shape[1] // width
    slabs = owned * width // residues

    @pl.when(step == 0)
    def prepare():
        relative_scr[...] = jnp.zeros_like(relative_scr)
        relative_scr[0:heads, 0:bins] = relative_ref[...]
        table = relative_scr[...]
        row = offsets_ref[...]
        column = jnp.broadcast_to(row, (LANES, residues)).T
        for block in range(residues // LANES):
            lanes = slice(block * LANES, (block + 1) * LANES)
            start, stop = block * LANES, (block + 1) * LANES
            low = max(0, (start - REACH + 1) // 8 * 8)
            high = min(residues, -(-(stop + REACH) // 8) * 8)
            for tile in range(low, high, 8):
                rows = slice(tile, tile + 8)
                index = jnp.clip(row[:, lanes] - column[rows], -REACH, REACH) + REACH
                for head in range(heads):
                    source = jnp.broadcast_to(table[head : head + 1, :], (8, LANES))
                    bias_scr[head, rows, lanes] = jnp.take_along_axis(source, index, axis=1)
            for head in range(heads):
                if low:
                    after = table[head : head + 1, 2 * REACH : 2 * REACH + 1]
                    bias_scr[head, 0:low, lanes] = jnp.broadcast_to(after, (low, LANES))
                if high < residues:
                    before = table[head : head + 1, 0:1]
                    bias_scr[head, high:, lanes] = jnp.broadcast_to(before, (residues - high, LANES))
        embed_scr[...] = jnp.zeros_like(embed_scr)
        embed = embed_ref[...]
        high = embed.astype(BF16)
        rest = embed - high.astype(F32)
        middle = rest.astype(BF16)
        low = (rest - middle.astype(F32)).astype(BF16)
        for part, piece in enumerate((high, middle, low)):
            embed_scr[part * padded : part * padded + classes, :] = piece
        left_scr[...] = jnp.zeros_like(left_scr)
        for tile in range(LANES // width):
            left_scr[tile, tile * width : (tile + 1) * width, :] = left_ref[...]
        target_row = lax.broadcasted_iota(jnp.int32, gather_scr.shape, 0)
        gather_scr[...] = (
            target_row % owners * owned + target_row // owners
            == lax.broadcasted_iota(jnp.int32, gather_scr.shape, 1)
        ).astype(F32).astype(BF16)
        place = lax.broadcasted_iota(jnp.int32, (1, LANES), 1) // head_size
        for member in range(packed):
            ones = jnp.where(place == member, jnp.ones((), BF16), jnp.zeros((), BF16))
            for k in range(together):
                mixer_scr[k, member * residues : (member + 1) * residues, LANES:] = jnp.broadcast_to(
                    ones, (residues, LANES)
                )

    place = lax.broadcasted_iota(jnp.int32, (1, LANES), 1) // head_size
    blank = jnp.zeros((), BF16)
    members = range(together)
    rows = [step * together + k for k in members]
    initial, query, keys, values, gates = [], [], [], [], []
    classes_iota = lax.broadcasted_iota(jnp.int32, (padded, residues), 0)
    for k in members:
        tokens = tokens_ref[pl.ds(rows[k], 1), :]
        onehot = (classes_iota == tokens).astype(F32).astype(BF16)
        onehot = jnp.concatenate([onehot, onehot, onehot], axis=0)
        initial.append(dot(onehot, embed_scr[...], ((0,), (0,))) + target_ref[...])
    both_initial = jnp.concatenate(initial, axis=0)
    both_normed = normalize(both_initial, gain_ref[...]).astype(BF16)
    spans = [slice(k * residues, (k + 1) * residues) for k in members]
    product = dot(both_normed, query_ref[...], ((1,), (0,)))
    product = (product * (1.0 / head_size**0.5)).astype(BF16)
    query = [product[span] for span in spans]
    product = dot(both_normed, key_ref[...], ((1,), (0,))).astype(BF16)
    keys = [product[span] for span in spans]
    product = dot(both_normed, value_ref[...], ((1,), (0,))).astype(BF16)
    values = [product[span] for span in spans]
    mixed = [[] for _ in members]
    for group in range(groups):
        lanes = slice(group * LANES, (group + 1) * LANES)
        for member in range(packed):
            mine = place == member
            columns = slice(member * residues, (member + 1) * residues)
            for k in members:
                one_query = jnp.where(mine, query[k][:, lanes], blank)
                scores = dot(one_query, keys[k][:, lanes], ((1,), (1,)))
                scores = scores + bias_scr[group * packed + member]
                expo = jnp.exp(scores - jnp.max(scores, axis=-1, keepdims=True))
                weights_scr[k, :, columns] = expo.astype(BF16)
                mixer_scr[k, columns, 0:LANES] = jnp.where(mine, values[k][:, lanes], blank)
        for k in members:
            both = dot(weights_scr[k], mixer_scr[k], ((1,), (0,)))
            mixed[k].append(both[:, :LANES] / both[:, LANES:])
    gates = jax.nn.sigmoid(dot(both_normed, gate_ref[...], ((1,), (0,))) + gate_bias_ref[...])
    whole = jnp.concatenate([jnp.concatenate(mixed[k], axis=1) for k in members], axis=0)
    whole = (whole * gates).astype(BF16)
    updated = both_initial + dot(whole, output_ref[...], ((1,), (0,)))
    normed_two = normalize(updated, gain_two_ref[...]).astype(BF16)
    for k in members:
        updated_ref[k] = updated[spans[k]]
        narrow_scr[rows[k]] = normed_two[spans[k]]

    @pl.when(step == pl.num_programs(0) - 1)
    def finish():
        for k in range(count):
            narrow = narrow_scr[k]
            sorted_rows = dot(gather_scr[...], narrow, ((1,), (0,))).astype(BF16)
            sorted_scr[:, k] = sorted_rows.reshape(owned, owners, features)
            right = dot(right_ref[...], narrow, ((1,), (1,)))
            for tile in range(residues // LANES):
                lanes = slice(tile * LANES, (tile + 1) * LANES)
                factor_scr[tile, pl.ds(k, width, stride=count), :] = right[:, lanes]
        fold = LANES // width
        for tile in range(owned // fold):
            total = jnp.zeros((count * owners, LANES), F32)
            for place in range(fold):
                one = sorted_scr[tile * fold + place].reshape(count * owners, features)
                total += dot(one, left_scr[place], ((1,), (1,)))
            owner_scr[tile] = total
        right = jnp.concatenate([factor_scr[t] for t in range(residues // LANES)], axis=1)
        right = right.astype(BF16).reshape(width, count, residues)
        mine = lax.axis_index("wide") // inner
        per = residues // LANES
        for shift, message_ref in enumerate(message_refs):
            target = meet(mine, shift, outer) * inner
            message_ref[0:width] = right
            for k in range(inner):
                for slab in range(slabs):
                    block = [
                        owner_scr[slab * per + t, pl.ds(target + k, count, stride=owners), :] for t in range(per)
                    ]
                    message_ref[width + k * slabs + slab] = jnp.concatenate(block, axis=1).astype(BF16)


def attention(operands, heads, owners, outer):
    tokens, _, target, embed, _, query_weight = operands[:6]
    _, right_weight = operands[13:15]
    count, residues = tokens.shape
    features = target.shape[1]
    head_size = query_weight.shape[1] // heads
    packed = LANES // head_size
    width = right_weight.shape[0]
    owned = residues // owners
    padded = -(-embed.shape[0] // 32) * 32
    together = math.gcd(count, max(1, ROWS // residues))
    whole = lambda x: pl.BlockSpec(x.shape, lambda s, n=x.ndim: (0,) * n)
    slabs = owned * width // residues
    message = (width + owners // outer * slabs, count, residues)
    outs = (jax.ShapeDtypeStruct((count, residues, features), F32),) + (
        jax.ShapeDtypeStruct(message, BF16),
    ) * outer
    scratch = [
        ((heads, residues, residues), F32),
        ((heads, LANES), F32),
        ((3 * padded, features), BF16),
        ((LANES // width, LANES, features), BF16),
        ((together, residues, packed * residues), BF16),
        ((together, packed * residues, 2 * LANES), BF16),
        ((residues // LANES, width * count, LANES), F32),
        ((owned * width // LANES, owners * count, LANES), F32),
        ((residues, residues), BF16),
        ((count, residues, features), BF16),
        ((owned, count, owners, features), BF16),
    ]
    return pl.pallas_call(
        functools.partial(attention_kernel, heads, owners, outer, together),
        grid=(count // together,),
        in_specs=[whole(x) for x in operands],
        out_specs=(pl.BlockSpec((together, residues, features), lambda s: (s, 0, 0)),)
        + tuple(whole(x) for x in outs[1:]),
        out_shape=outs,
        scratch_shapes=[pltpu.VMEM(shape, dtype) for shape, dtype in scratch],
        cost_estimate=pl.CostEstimate(
            flops=count * residues * (8 * features * features + 8 * heads * residues * LANES),
            transcendentals=count * heads * residues * residues,
            bytes_accessed=4 * count * residues * features,
        ),
        name="attention",
    )(*operands)


def spread(messages, devices):
    outer = len(messages)
    inner = devices // outer
    core = 2 if inner % 2 == 0 else 1

    def move(piece, target):
        return lax.ppermute(piece, "wide", [(d, target(d)) for d in range(devices)])

    pieces = [messages[0]] + [
        move(message, lambda d, k=shift: meet(d // inner, k, outer) * inner + d % inner)
        for shift, message in enumerate(messages)
        if shift
    ]
    for axis, stride in ((inner // core, core), (core, 1)):
        pieces = pieces + [
            move(
                piece,
                lambda d, k=shift: d + ((d // stride + k) % axis - d // stride % axis) * stride,
            )
            for shift in range(1, axis)
            for piece in pieces
        ]
    return pieces


def order_kernel(weight_ref, own_ref, out_ref, kept_ref, wide_scr, sem):
    width = round(weight_ref.shape[0] ** 0.5)
    copy = pltpu.make_async_copy(own_ref, kept_ref, sem)
    copy.start()
    wide_scr[...] = weight_ref[...].astype(F32)
    for e in range(width):
        out_ref[:, e * width : (e + 1) * width] = wide_scr[pl.ds(e, width, stride=width), :].T.astype(BF16)
    copy.wait()


def ordered(weight, own):
    shape = weight.shape[::-1]
    return pl.pallas_call(
        order_kernel,
        in_specs=[pl.BlockSpec(weight.shape, lambda: (0, 0)), pl.BlockSpec(memory_space=pl.ANY)],
        out_shape=(jax.ShapeDtypeStruct(shape, BF16), jax.ShapeDtypeStruct(own.shape, own.dtype)),
        scratch_shapes=[pltpu.VMEM(weight.shape, F32), pltpu.SemaphoreType.DMA],
        compiler_params=pltpu.CompilerParams(vmem_limit_bytes=8 * 2**20),
        cost_estimate=pl.CostEstimate(flops=0, transcendentals=0, bytes_accessed=4 * math.prod(shape)),
        name="order",
    )(weight, own)


def pair_kernel(inner, blocks, weight_ref, bias_ref, *rest_refs):
    pieces = len(rest_refs) - 5
    piece_refs = rest_refs[:pieces]
    out_hbm, flat_scr, outer_scr, out_scr, sems = rest_refs[pieces:]
    slabs, count, residues = piece_refs[0].shape
    block, depth = out_scr.shape[1], outer_scr.shape[1]
    width = round(depth**0.5)
    slabs = (slabs - width) // inner
    mine = lax.rem(lax.axis_index("wide"), inner) * slabs + width
    for slab in range(slabs):
        left = jnp.concatenate([ref[mine + slab].astype(F32) for ref in piece_refs], axis=0)
        flat_scr[slab * residues : (slab + 1) * residues, :] = left.T.astype(BF16)
    total = float(pieces * count)
    copies = [
        pltpu.make_async_copy(out_scr.at[n], out_hbm.at[pl.ds(n * block, block)], sems.at[n])
        for n in range(blocks)
    ]
    for n in range(blocks):
        rows = slice(n * block * width, (n + 1) * block * width)
        for e in range(width):
            right = jnp.concatenate([ref[e].astype(F32) for ref in piece_refs], axis=0).astype(BF16)
            product = dot(flat_scr[rows, :], right, ((1,), (0,))).astype(BF16)
            outer_scr[:, e * width : (e + 1) * width, :] = product.reshape(block, width, residues)
        for i in range(block):
            projected = dot(weight_ref[...], outer_scr[i], ((1,), (0,)))
            out_scr[n, i] = projected.T * (1.0 / total) + bias_ref[...]
        copies[n].start()
    for copy in copies:
        copy.wait()


def pair_features(pieces, weight, bias, count, inner, owned, blocks):
    residues = pieces[0].shape[2]
    channels = weight.shape[0]
    width = round(weight.shape[1] ** 0.5)
    block = owned // blocks
    scratch = [
        ((owned * width, len(pieces) * count), BF16),
        ((block, width * width, residues), BF16),
        ((blocks, block, residues, channels), F32),
    ]
    used = room(scratch) + 2 * room([(weight.shape, BF16)])
    vmem = pl.BlockSpec(memory_space=pltpu.VMEM)
    return pl.pallas_call(
        functools.partial(pair_kernel, inner, blocks),
        in_specs=[vmem] * (2 + len(pieces)),
        out_specs=pl.BlockSpec(memory_space=pl.ANY),
        out_shape=jax.ShapeDtypeStruct((owned, residues, channels), F32),
        scratch_shapes=[pltpu.VMEM(shape, dtype) for shape, dtype in scratch]
        + [pltpu.SemaphoreType.DMA((blocks,))],
        compiler_params=pltpu.CompilerParams(vmem_limit_bytes=used + 12 * 2**20),
        name="pair",
    )(weight, bias.reshape(1, -1), *pieces)


def shards(
    alignment_token_ids,
    residue_index_offsets,
    target_residue_feature,
    token_embedding_table,
    attention_norm_gain,
    query_weight,
    key_weight,
    value_weight,
    gate_weight,
    gate_offset_bias,
    output_weight,
    relative_position_table,
    product_norm_gain,
    left_weight,
    right_weight,
    pair_weight,
    pair_projection_bias,
):
    devices = lax.axis_size("wide")
    inner = nearest(devices)
    sequences, residues = alignment_token_ids.shape
    operands = (
        alignment_token_ids,
        residue_index_offsets.reshape(1, -1),
        target_residue_feature,
        token_embedding_table,
        attention_norm_gain.reshape(1, -1),
        query_weight,
        key_weight,
        value_weight,
        gate_weight,
        gate_offset_bias.reshape(1, -1),
        output_weight,
        relative_position_table.T,
        product_norm_gain.reshape(1, -1),
        left_weight.T,
        right_weight.T,
    )
    heads = relative_position_table.shape[1]
    updated, *messages = attention(operands, heads, devices, devices // inner)
    pieces = spread(messages, devices)
    weight, pieces[0] = ordered(pair_weight, messages[0])
    pair = pair_features(
        pieces,
        weight,
        pair_projection_bias,
        sequences,
        inner,
        residues // devices,
        2,
    )
    return (updated, pair)


def solution(mesh):
    placed = (P(("groups", "wide"), None), P("groups"), P("groups", None)) + (P(),) * 14
    return jax.shard_map(
        shards,
        mesh=mesh,
        in_specs=placed,
        out_specs=(P(("groups", "wide"), None, None), P(("groups", "wide"), None, None)),
        check_vma=False,
    )
```

```python
import functools
import math

import jax
import jax.numpy as jnp
from jax import lax
from jax.experimental import pallas as pl
from jax.experimental.pallas import tpu as pltpu
from jax.sharding import PartitionSpec as P


REACH = 32
LANES = 128
ROWS = 1024
F32 = jnp.float32
BF16 = jnp.bfloat16


def dot(a, b, axes):
    return lax.dot_general(a, b, (axes, ((), ())), preferred_element_type=F32)


def normalize(values, gain):
    center = jnp.mean(values, axis=-1, keepdims=True)
    centred = values - center
    spread = jnp.mean(centred * centred, axis=-1, keepdims=True)
    return centred * lax.rsqrt(spread + 1e-05) * gain


def meet(place, shift, size):
    if size & (size - 1):
        return (place + shift) % size
    return place ^ shift


def nearest(devices):
    core = 2 if devices % 2 == 0 else 1
    return 2 * core if devices % (2 * core) == 0 else core


def room(shapes):
    total = 0
    for shape, dtype in shapes:
        total += math.prod(shape) * jnp.dtype(dtype).itemsize
    return total


def attention_kernel(heads, owners, outer, together, *refs):
    (
        tokens_ref,
        offsets_ref,
        target_hbm,
        embed_ref,
        gain_ref,
        query_hbm,
        key_hbm,
        value_hbm,
        gate_hbm,
        gate_bias_ref,
        output_hbm,
        relative_ref,
        gain_two_ref,
        left_ref,
        right_ref,
    ) = refs[:15]
    updated_ref, *rest_refs = refs[15:]
    message_refs = rest_refs[:outer]
    (
        bias_scr,
        relative_scr,
        embed_scr,
        left_scr,
        weights_scr,
        mixer_scr,
        factor_scr,
        owner_scr,
        gather_scr,
        narrow_scr,
        sorted_scr,
        target_ref,
        query_ref,
        key_ref,
        value_ref,
        gate_ref,
        output_ref,
        sems,
    ) = rest_refs[outer:]
    moved = (
        (target_hbm, target_ref),
        (query_hbm, query_ref),
        (key_hbm, key_ref),
        (value_hbm, value_ref),
        (gate_hbm, gate_ref),
        (output_hbm, output_ref),
    )
    copies = [pltpu.make_async_copy(a, b, sems.at[n]) for n, (a, b) in enumerate(moved)]
    step = pl.program_id(0)
    residues, features = target_ref.shape
    head_size = query_ref.shape[1] // heads
    packed = LANES // head_size
    groups = heads // packed
    classes = embed_ref.shape[0]
    padded = embed_scr.shape[0] // 3
    width = right_ref.shape[0]
    bins = relative_ref.shape[1]
    inner = owners // outer
    core = 2 if inner % 2 == 0 else 1
    owned = residues // owners
    count = factor_scr.shape[1] // width
    slabs = owned * width // residues

    @pl.when(step == 0)
    def prepare():
        for copy in copies:
            copy.start()
        relative_scr[...] = jnp.zeros_like(relative_scr)
        relative_scr[0:heads, 0:bins] = relative_ref[...]
        table = relative_scr[...]
        row = offsets_ref[...]
        column = jnp.broadcast_to(row, (LANES, residues)).T
        for block in range(residues // LANES):
            lanes = slice(block * LANES, (block + 1) * LANES)
            start, stop = block * LANES, (block + 1) * LANES
            low = max(0, (start - REACH + 1) // 8 * 8)
            high = min(residues, -(-(stop + REACH) // 8) * 8)
            for tile in range(low, high, 8):
                rows = slice(tile, tile + 8)
                index = jnp.clip(row[:, lanes] - column[rows], -REACH, REACH) + REACH
                for head in range(heads):
                    source = jnp.broadcast_to(table[head : head + 1, :], (8, LANES))
                    bias_scr[head, rows, lanes] = jnp.take_along_axis(source, index, axis=1)
            for head in range(heads):
                if low:
                    after = table[head : head + 1, 2 * REACH : 2 * REACH + 1]
                    bias_scr[head, 0:low, lanes] = jnp.broadcast_to(after, (low, LANES))
                if high < residues:
                    before = table[head : head + 1, 0:1]
                    bias_scr[head, high:, lanes] = jnp.broadcast_to(before, (residues - high, LANES))
        embed_scr[...] = jnp.zeros_like(embed_scr)
        embed = embed_ref[...]
        high = embed.astype(BF16)
        rest = embed - high.astype(F32)
        middle = rest.astype(BF16)
        low = (rest - middle.astype(F32)).astype(BF16)
        for part, piece in enumerate((high, middle, low)):
            embed_scr[part * padded : part * padded + classes, :] = piece
        left_scr[...] = jnp.zeros_like(left_scr)
        for tile in range(LANES // width):
            left_scr[tile, tile * width : (tile + 1) * width, :] = left_ref[...]
        target_row = lax.broadcasted_iota(jnp.int32, gather_scr.shape, 0)
        gather_scr[...] = (
            target_row % owners * owned + target_row // owners
            == lax.broadcasted_iota(jnp.int32, gather_scr.shape, 1)
        ).astype(F32).astype(BF16)
        place = lax.broadcasted_iota(jnp.int32, (1, LANES), 1) // head_size
        for member in range(packed):
            ones = jnp.where(place == member, jnp.ones((), BF16), jnp.zeros((), BF16))
            for k in range(together):
                mixer_scr[k, member * residues : (member + 1) * residues, LANES:] = jnp.broadcast_to(
                    ones, (residues, LANES)
                )
        for copy in copies:
            copy.wait()

    place = lax.broadcasted_iota(jnp.int32, (1, LANES), 1) // head_size
    blank = jnp.zeros((), BF16)
    members = range(together)
    rows = [step * together + k for k in members]
    initial, query, keys, values, gates = [], [], [], [], []
    classes_iota = lax.broadcasted_iota(jnp.int32, (padded, residues), 0)
    for k in members:
        tokens = tokens_ref[pl.ds(rows[k], 1), :]
        onehot = (classes_iota == tokens).astype(F32).astype(BF16)
        onehot = jnp.concatenate([onehot, onehot, onehot], axis=0)
        initial.append(dot(onehot, embed_scr[...], ((0,), (0,))) + target_ref[...])
    both_initial = jnp.concatenate(initial, axis=0)
    both_normed = normalize(both_initial, gain_ref[...]).astype(BF16)
    spans = [slice(k * residues, (k + 1) * residues) for k in members]
    product = dot(both_normed, query_ref[...], ((1,), (0,)))
    product = (product * (1.0 / head_size**0.5)).astype(BF16)
    query = [product[span] for span in spans]
    product = dot(both_normed, key_ref[...], ((1,), (0,))).astype(BF16)
    keys = [product[span] for span in spans]
    product = dot(both_normed, value_ref[...], ((1,), (0,))).astype(BF16)
    values = [product[span] for span in spans]
    mixed = [[] for _ in members]
    for group in range(groups):
        lanes = slice(group * LANES, (group + 1) * LANES)
        for member in range(packed):
            mine = place == member
            columns = slice(member * residues, (member + 1) * residues)
            for k in members:
                one_query = jnp.where(mine, query[k][:, lanes], blank)
                scores = dot(one_query, keys[k][:, lanes], ((1,), (1,)))
                scores = scores + bias_scr[group * packed + member]
                expo = jnp.exp(scores - jnp.max(scores, axis=-1, keepdims=True))
                weights_scr[k, :, columns] = expo.astype(BF16)
                mixer_scr[k, columns, 0:LANES] = jnp.where(mine, values[k][:, lanes], blank)
        for k in members:
            both = dot(weights_scr[k], mixer_scr[k], ((1,), (0,)))
            mixed[k].append(both[:, :LANES] / both[:, LANES:])
    gates = jax.nn.sigmoid(dot(both_normed, gate_ref[...], ((1,), (0,))) + gate_bias_ref[...])
    whole = jnp.concatenate([jnp.concatenate(mixed[k], axis=1) for k in members], axis=0)
    whole = (whole * gates).astype(BF16)
    updated = both_initial + dot(whole, output_ref[...], ((1,), (0,)))
    normed_two = normalize(updated, gain_two_ref[...]).astype(BF16)
    for k in members:
        updated_ref[k] = updated[spans[k]]
        narrow_scr[rows[k]] = normed_two[spans[k]]

    @pl.when(step == pl.num_programs(0) - 1)
    def finish():
        for k in range(count):
            narrow = narrow_scr[k]
            sorted_rows = dot(gather_scr[...], narrow, ((1,), (0,))).astype(BF16)
            sorted_scr[:, k] = sorted_rows.reshape(owned, owners, features)
            right = dot(right_ref[...], narrow, ((1,), (1,)))
            for tile in range(residues // LANES):
                lanes = slice(tile * LANES, (tile + 1) * LANES)
                factor_scr[tile, pl.ds(k, width, stride=count), :] = right[:, lanes]
        fold = LANES // width
        for tile in range(owned // fold):
            total = jnp.zeros((count * owners, LANES), F32)
            for place in range(fold):
                one = sorted_scr[tile * fold + place].reshape(count * owners, features)
                total += dot(one, left_scr[place], ((1,), (1,)))
            owner_scr[tile] = total
        right = jnp.concatenate([factor_scr[t] for t in range(residues // LANES)], axis=1)
        right = right.astype(BF16).reshape(width, count, residues)
        me = lax.axis_index("wide")
        near = lax.rem(me, inner) // core * core
        per = residues // LANES
        edge = core * slabs
        for shift, message_ref in enumerate(message_refs):
            target = meet(me // inner, shift, outer) * inner
            message_ref[edge : edge + width] = right
            for k in range(inner):
                owner = target + lax.rem(near + k, inner)
                place = k * slabs if k < core else width + k * slabs
                for slab in range(slabs):
                    block = [
                        owner_scr[slab * per + t, pl.ds(owner, count, stride=owners), :] for t in range(per)
                    ]
                    message_ref[place + slab] = jnp.concatenate(block, axis=1).astype(BF16)


def attention(operands, heads, owners, outer):
    tokens, _, target, embed, _, query_weight = operands[:6]
    _, right_weight = operands[13:15]
    count, residues = tokens.shape
    features = target.shape[1]
    head_size = query_weight.shape[1] // heads
    packed = LANES // head_size
    width = right_weight.shape[0]
    owned = residues // owners
    padded = -(-embed.shape[0] // 32) * 32
    together = math.gcd(count, max(1, ROWS // residues))
    whole = lambda x: pl.BlockSpec(x.shape, lambda s, n=x.ndim: (0,) * n)
    slabs = owned * width // residues
    message = (width + owners // outer * slabs, count, residues)
    outs = (jax.ShapeDtypeStruct((count, residues, features), F32),) + (
        jax.ShapeDtypeStruct(message, BF16),
    ) * outer
    scratch = [
        ((heads, residues, residues), F32),
        ((heads, LANES), F32),
        ((3 * padded, features), BF16),
        ((LANES // width, LANES, features), BF16),
        ((together, residues, packed * residues), BF16),
        ((together, packed * residues, 2 * LANES), BF16),
        ((residues // LANES, width * count, LANES), F32),
        ((owned * width // LANES, owners * count, LANES), F32),
        ((residues, residues), BF16),
        ((count, residues, features), BF16),
        ((owned, count, owners, features), BF16),
    ]
    moved = (2, 5, 6, 7, 8, 10)
    in_specs = [
        pl.BlockSpec(memory_space=pl.ANY) if n in moved else whole(x) for n, x in enumerate(operands)
    ]
    return pl.pallas_call(
        functools.partial(attention_kernel, heads, owners, outer, together),
        grid=(count // together,),
        in_specs=in_specs,
        out_specs=(pl.BlockSpec((together, residues, features), lambda s: (s, 0, 0)),)
        + tuple(whole(x) for x in outs[1:]),
        out_shape=outs,
        scratch_shapes=[pltpu.VMEM(shape, dtype) for shape, dtype in scratch]
        + [pltpu.VMEM(operands[n].shape, operands[n].dtype) for n in moved]
        + [pltpu.SemaphoreType.DMA((len(moved),))],
        cost_estimate=pl.CostEstimate(
            flops=count * residues * (8 * features * features + 8 * heads * residues * LANES),
            transcendentals=count * heads * residues * residues,
            bytes_accessed=4 * count * residues * features,
        ),
        name="attention",
    )(*operands)


def spread(messages, devices, edge):
    outer = len(messages)
    inner = devices // outer
    core = 2 if inner % 2 == 0 else 1

    def move(piece, target):
        return lax.ppermute(piece, "wide", [(d, target(d)) for d in range(devices)])

    pieces = [messages[0]] + [
        move(message, lambda d, k=shift: meet(d // inner, k, outer) * inner + d % inner)
        for shift, message in enumerate(messages)
        if shift
    ]
    for name, axis, stride in (("y", inner // core, core), ("c", core, 1)):
        pieces = pieces + [
            move(
                piece[edge:] if name == "y" else piece,
                lambda d, k=shift: d + ((d // stride + k) % axis - d // stride % axis) * stride,
            )
            for shift in range(1, axis)
            for piece in pieces
        ]
    return pieces


def order_kernel(weight_ref, own_ref, out_ref, kept_ref, wide_scr, sem):
    width = round(weight_ref.shape[0] ** 0.5)
    copy = pltpu.make_async_copy(own_ref, kept_ref, sem)
    copy.start()
    wide_scr[...] = weight_ref[...].astype(F32)
    for e in range(width):
        out_ref[:, e * width : (e + 1) * width] = wide_scr[pl.ds(e, width, stride=width), :].T.astype(BF16)
    copy.wait()


def ordered(weight, own):
    shape = weight.shape[::-1]
    return pl.pallas_call(
        order_kernel,
        in_specs=[pl.BlockSpec(weight.shape, lambda: (0, 0)), pl.BlockSpec(memory_space=pl.ANY)],
        out_shape=(jax.ShapeDtypeStruct(shape, BF16), jax.ShapeDtypeStruct(own.shape, own.dtype)),
        scratch_shapes=[pltpu.VMEM(weight.shape, F32), pltpu.SemaphoreType.DMA],
        compiler_params=pltpu.CompilerParams(vmem_limit_bytes=8 * 2**20),
        cost_estimate=pl.CostEstimate(flops=0, transcendentals=0, bytes_accessed=4 * math.prod(shape)),
        name="order",
    )(weight, own)


def pair_kernel(inner, blocks, weight_ref, bias_ref, *rest_refs):
    pieces = len(rest_refs) - 5
    piece_refs = rest_refs[:pieces]
    out_hbm, flat_scr, outer_scr, out_scr, sems = rest_refs[pieces:]
    slabs, count, residues = piece_refs[0].shape
    block, depth = out_scr.shape[1], outer_scr.shape[1]
    width = round(depth**0.5)
    longest = slabs
    slabs = (slabs - width) // inner
    core = 2 if inner % 2 == 0 else 1
    mine = lax.rem(lax.axis_index("wide"), core) * slabs
    starts = [core * slabs if ref.shape[0] == longest else 0 for ref in piece_refs]
    places = [mine if start else mine + width for start in starts]
    for slab in range(slabs):
        left = jnp.concatenate([
            ref[place + slab].astype(F32) for ref, place in zip(piece_refs, places)
        ], axis=0)
        flat_scr[slab * residues : (slab + 1) * residues, :] = left.T.astype(BF16)
    total = float(pieces * count)
    copies = [
        pltpu.make_async_copy(out_scr.at[n], out_hbm.at[pl.ds(n * block, block)], sems.at[n])
        for n in range(blocks)
    ]
    for n in range(blocks):
        rows = slice(n * block * width, (n + 1) * block * width)
        for e in range(width):
            right = jnp.concatenate([ref[start + e].astype(F32) for ref, start in zip(piece_refs, starts)], axis=0).astype(BF16)
            product = dot(flat_scr[rows, :], right, ((1,), (0,))).astype(BF16)
            outer_scr[:, e * width : (e + 1) * width, :] = product.reshape(block, width, residues)
        for i in range(block):
            projected = dot(weight_ref[...], outer_scr[i], ((1,), (0,)))
            out_scr[n, i] = projected.T * (1.0 / total) + bias_ref[...]
        copies[n].start()
    for copy in copies:
        copy.wait()


def pair_features(pieces, weight, bias, count, inner, owned, blocks):
    residues = pieces[0].shape[2]
    channels = weight.shape[0]
    width = round(weight.shape[1] ** 0.5)
    block = owned // blocks
    scratch = [
        ((owned * width, len(pieces) * count), BF16),
        ((block, width * width, residues), BF16),
        ((blocks, block, residues, channels), F32),
    ]
    used = room(scratch) + 2 * room([(weight.shape, BF16)])
    vmem = pl.BlockSpec(memory_space=pltpu.VMEM)
    return pl.pallas_call(
        functools.partial(pair_kernel, inner, blocks),
        in_specs=[vmem] * (2 + len(pieces)),
        out_specs=pl.BlockSpec(memory_space=pl.ANY),
        out_shape=jax.ShapeDtypeStruct((owned, residues, channels), F32),
        scratch_shapes=[pltpu.VMEM(shape, dtype) for shape, dtype in scratch]
        + [pltpu.SemaphoreType.DMA((blocks,))],
        compiler_params=pltpu.CompilerParams(vmem_limit_bytes=used + 12 * 2**20),
        name="pair",
    )(weight, bias.reshape(1, -1), *pieces)


def shards(
    alignment_token_ids,
    residue_index_offsets,
    target_residue_feature,
    token_embedding_table,
    attention_norm_gain,
    query_weight,
    key_weight,
    value_weight,
    gate_weight,
    gate_offset_bias,
    output_weight,
    relative_position_table,
    product_norm_gain,
    left_weight,
    right_weight,
    pair_weight,
    pair_projection_bias,
):
    devices = lax.axis_size("wide")
    inner = nearest(devices)
    sequences, residues = alignment_token_ids.shape
    operands = (
        alignment_token_ids,
        residue_index_offsets.reshape(1, -1),
        target_residue_feature,
        token_embedding_table,
        attention_norm_gain.reshape(1, -1),
        query_weight,
        key_weight,
        value_weight,
        gate_weight,
        gate_offset_bias.reshape(1, -1),
        output_weight,
        relative_position_table.T,
        product_norm_gain.reshape(1, -1),
        left_weight.T,
        right_weight.T,
    )
    heads = relative_position_table.shape[1]
    updated, *messages = attention(operands, heads, devices, devices // inner)
    core = 2 if inner % 2 == 0 else 1
    edge = core * (residues // devices * left_weight.shape[1] // residues)
    pieces = spread(messages, devices, edge)
    weight, pieces[0] = ordered(pair_weight, messages[0])
    pair = pair_features(
        pieces,
        weight,
        pair_projection_bias,
        sequences,
        inner,
        residues // devices,
        4,
    )
    return (updated, pair)


def solution(mesh):
    placed = (P(("groups", "wide"), None), P("groups"), P("groups", None)) + (P(),) * 14
    return jax.shard_map(
        shards,
        mesh=mesh,
        in_specs=placed,
        out_specs=(P(("groups", "wide"), None, None), P(("groups", "wide"), None, None)),
        check_vma=False,
    )
```
